32 devices in a mesh: lat: 4 (over z), lon: 8 (over y, x, core).
Axes of the slice: x: 2, y: 2, z: 4, core: 2. Of those that a mesh axis runs over, the one named last changes fastest.
Arguments:
- mesh_latent: bfloat16 [32, 64, 512], P('lat', 'lon'), may hold values from -6 to 6
- grid_cotangent: bfloat16 [32768, 512], P(('lat', 'lon')), may hold values from -6 to 6
- w_source: bfloat16 [512, 512], replicated, may hold values from -0.25 to 0.25
- w_target: bfloat16 [512, 512], replicated, may hold values from -0.25 to 0.25
- w_node: bfloat16 [512, 512], replicated, may hold values from -0.25 to 0.25
- w_coarse: bfloat16 [512, 512], replicated, may hold values from -0.25 to 0.25
- w_decode: bfloat16 [512, 512], replicated, may hold values from -0.25 to 0.25
- neighbour_codes: int32 [6, 32, 64], P(None, 'lat', 'lon'), may hold values from 0 to 8, as said below
- coarse_ids: int32 [32, 64, 1], P('lat', 'lon'), may hold values from 0 to 641
- edge_source: int32 [98304], P(('lat', 'lon')), may hold values from 0 to 63
- edge_target: int32 [98304], P(('lat', 'lon')), may hold values from 0 to 1023
- edge_owner: int32 [768, 1], P(('lat', 'lon')), may hold values from 0 to 7, as said below
Outputs:
- mesh_out: bfloat16 [32, 64, 512], P('lat', 'lon')
- grid_out: bfloat16 [32768, 512], P(('lat', 'lon'))
- clipped: float32 [5, 262144], P(None, ('lat', 'lon'))
The draws below stay inside these ranges and needn't reach their ends.
Inputs may be any that keep to these rules, and one draw needn't show every extreme that they name: `neighbour_codes`: code c names the row offset c // 3 - 1 and the column offset c % 3 - 1 and is never 4; the six codes of one node differ. `coarse_ids`: every coarse node has at least one mesh node. `edge_owner`: the owner of a block held by the device at longitude index b is b, or b - 1 or b + 1 on the periodic cycle of longitude indices. Among the 24 blocks of one device at most 3 name b - 1 and at most 3 name b + 1; in every draw some device receives 3 blocks from each of its two neighbours.
All inputs are finite; a program needn't handle non-finite values.
Results may differ from the reference program's by a relative error of at most 0.008.
Values may be sent and summed in bfloat16 or wider, within the bound.
A program may use at most 64 MiB of HBM per device.

```python
import jax
import jax.numpy as jnp
from jax import lax

D = 512
ROWS_DEV = 8
COLS_DEV = 8
GRID_DEV = 1024
BLOCK = 128
COARSE = 642
BLOCKS_DEV = 24
CAP = 3
MESH_ROWS = 32
MESH_COLS = 64
GRID = 32768
EDGES = 98304
N_LAT = 4
N_LON = 8
DEVICES = 32


def draw_neighbour_codes(key, part):
    scores = jax.random.randint(key, (N_LAT * ROWS_DEV, N_LON * COLS_DEV, 8), 0, 1 << 20) * 8 + jnp.arange(8, dtype=jnp.int32)
    order = jnp.argsort(scores, axis=-1, stable=True)[..., :6]
    codes = order + (order >= 4).astype(jnp.int32)
    return jnp.transpose(codes, (2, 0, 1)).astype(jnp.int32)


def draw_edge_owner(key, part):
    devices = N_LAT * N_LON
    base = jax.random.fold_in(key, 7)
    key_counts, key_star, key_order = jax.random.split(base, 3)
    counts = jax.random.randint(key_counts, (devices, 2), 0, CAP + 1).astype(jnp.int32)
    star = jax.random.randint(key_star, (), 0, devices).astype(jnp.int32)
    star_lat = star // N_LON
    star_lon = star % N_LON
    sender_left = star_lat * N_LON + (star_lon + N_LON - 1) % N_LON
    sender_right = star_lat * N_LON + (star_lon + 1) % N_LON
    dev_ids = jnp.arange(devices, dtype=jnp.int32)
    to_left = jnp.where(dev_ids == sender_right, CAP, counts[:, 0])
    to_right = jnp.where(dev_ids == sender_left, CAP, counts[:, 1])
    scores = jax.random.randint(key_order, (devices, BLOCKS_DEV), 0, 1 << 20) * BLOCKS_DEV + jnp.arange(BLOCKS_DEV, dtype=jnp.int32)[None]
    order = jnp.argsort(scores, axis=1, stable=True)
    ranks = jnp.argsort(order, axis=1, stable=True).astype(jnp.int32)
    offset = jnp.where(ranks < to_left[:, None], -1, jnp.where(ranks < (to_left + to_right)[:, None], 1, 0))
    lon_ids = dev_ids % N_LON
    owner = (lon_ids[:, None] + offset + N_LON) % N_LON
    return owner.reshape(devices * BLOCKS_DEV, 1).astype(jnp.int32)


def with_ends(array, rng, low, high):
    longest = array.shape.index(max(array.shape))
    spots = []
    for shift in (0, 1):
        where = [jax.random.randint(jax.random.fold_in(rng, axis), (), 0, length) for axis, length in enumerate(array.shape)]
        where[longest] = (where[longest] + shift) % array.shape[longest]
        spots.append(tuple(where))
    return array.at[spots[0]].set(low).at[spots[1]].set(high)


def block_levels(key, extent, shards, low, top_value):
    gain, own = 1.0, jax.random.fold_in(key, 6)
    for axis_at, parts in shards:
        draws = jnp.exp(jax.random.uniform(jax.random.fold_in(own, axis_at), (parts,), jnp.float32, low / len(shards), top_value / len(shards)))
        gain = gain * jnp.repeat(draws, extent[axis_at] // parts).reshape([-1 if axis == axis_at else 1 for axis in range(len(extent))])
    return gain


def different_ones(stream_key, rows, number_of, top, lift):
    sequence = jax.random.permutation(jax.random.fold_in(stream_key, 1), number_of)
    pull = sequence
    for power in range(3):
        pull = pull * pull // number_of
    pull = pull * lift // number_of
    lots = jax.random.randint(jax.random.fold_in(stream_key, 2), (rows, number_of), 0, 4096) + pull
    fixed_rows = jax.random.permutation(jax.random.fold_in(stream_key, 3), rows)[jnp.arange(number_of) % rows]
    lots = jnp.where(jnp.arange(rows)[:, None] == fixed_rows[None, :], 1 << 14, lots)
    merit = lots * number_of + jnp.arange(number_of)
    return lax.top_k(merit.astype(jnp.int32), top)[1].astype(jnp.int32)


def bell_draw(stream_key, dims, scale, reach, shards=(), held_as=jnp.bfloat16):
    entries = jax.random.normal(stream_key, dims, jnp.float32) * scale
    if len(shards) > 0:
        entries = block_levels(stream_key, dims, shards, -0.22, 0.18) * entries
    return jnp.clip(entries, min=-reach, max=reach).astype(held_as)


def setup_inputs(seed: int = 0) -> dict:
    arg_keys = jax.random.split(jax.random.key(seed), 13)
    return {
        "mesh_latent": bell_draw(arg_keys[0], (MESH_ROWS, MESH_COLS, D), 1.0, 6.0, ((0, 4), (1, 8))),
        "grid_cotangent": bell_draw(arg_keys[1], (GRID, D), 1.0, 6.0, ((0, 32),)),
        "w_source": bell_draw(arg_keys[2], (D, D), D ** -0.5, 0.25),
        "w_target": bell_draw(arg_keys[3], (D, D), D ** -0.5, 0.25),
        "w_node": bell_draw(arg_keys[4], (D, D), D ** -0.5, 0.25),
        "w_coarse": bell_draw(arg_keys[5], (D, D), D ** -0.5, 0.25),
        "w_decode": bell_draw(arg_keys[6], (D, D), D ** -0.5, 0.25),
        "neighbour_codes": draw_neighbour_codes(jax.random.fold_in(arg_keys[12], 71), 0),
        "coarse_ids": different_ones(arg_keys[8], MESH_ROWS * MESH_COLS, COARSE, 1, 12).reshape((MESH_ROWS, MESH_COLS, 1)),
        "edge_source": with_ends(jax.random.randint(arg_keys[9], (EDGES,), 0, ROWS_DEV * COLS_DEV), jax.random.fold_in(arg_keys[9], 1), 0, (ROWS_DEV * COLS_DEV) - 1).astype(jnp.int32),
        "edge_target": with_ends(jax.random.randint(arg_keys[10], (EDGES,), 0, GRID_DEV), jax.random.fold_in(arg_keys[10], 1), 0, GRID_DEV - 1).astype(jnp.int32),
        "edge_owner": draw_edge_owner(jax.random.fold_in(arg_keys[12], 71), 0),
    }


def silu_slope(value):
    sig = jax.nn.sigmoid(value)
    return sig * (1.0 + value * (1.0 - sig))

def reference(mesh_latent, grid_cotangent, w_source, w_target, w_node, w_coarse, w_decode, neighbour_codes, coarse_ids, edge_source, edge_target, edge_owner):
    height, breadth, width = mesh_latent.shape
    nodes = height * breadth
    wrapped = jnp.concatenate([mesh_latent[:, -1:], mesh_latent, mesh_latent[:, :1]], 1)
    padded = jnp.pad(wrapped, ((1, 1), (0, 0), (0, 0)))
    flat_pad = padded.reshape(-1, width)
    row_at = jnp.arange(height, dtype=jnp.int32)[None, :, None] + neighbour_codes // 3
    col_at = jnp.arange(breadth, dtype=jnp.int32)[None, None, :] + neighbour_codes % 3
    where_idx = (row_at * (breadth + 2) + col_at).reshape(-1).astype(jnp.int32)
    beside = jnp.take(flat_pad, where_idx, axis=0)
    latent = mesh_latent.reshape(nodes, width)
    toward = jnp.dot(latent, w_target, preferred_element_type=jnp.float32)
    edges_pre = jnp.dot(beside, w_source, preferred_element_type=jnp.float32).reshape(6, nodes, width) + toward[None]
    agg = lax.optimization_barrier(jnp.sum(jax.nn.silu(edges_pre), 0)).astype(jnp.bfloat16)
    onehot = (coarse_ids.reshape(nodes, 1) == jnp.arange(COARSE, dtype=jnp.int32)[None]).astype(jnp.bfloat16)
    pooled = jnp.dot(onehot.T, latent, preferred_element_type=jnp.float32)
    count = lax.optimization_barrier(jnp.sum(onehot.astype(jnp.float32), 0))
    coarse_in = (pooled * lax.rsqrt(count)[:, None]).astype(jnp.bfloat16)
    cpre = jnp.dot(coarse_in, w_coarse, preferred_element_type=jnp.float32)
    coarse_out = jax.nn.silu(cpre).astype(jnp.bfloat16)
    child = jnp.dot(onehot, coarse_out, preferred_element_type=jnp.float32)
    npre = jnp.dot(agg, w_node, preferred_element_type=jnp.float32) + child
    mesh_out = (latent.astype(jnp.float32) + jax.nn.silu(npre)).astype(jnp.bfloat16)
    per_dev = BLOCKS_DEV * BLOCK
    edge_ids = jnp.arange(EDGES, dtype=jnp.int32)
    device = edge_ids // per_dev
    lat_pos = device // N_LON
    lon_pos = device % N_LON
    owner = jnp.repeat(edge_owner[:, 0], BLOCK).astype(jnp.int32)
    src_row = lat_pos * ROWS_DEV + edge_source // COLS_DEV
    src_col = lon_pos * COLS_DEV + edge_source % COLS_DEV
    src_flat = (src_row * breadth + src_col).astype(jnp.int32)
    target = ((lat_pos * N_LON + owner) * GRID_DEV + edge_target).astype(jnp.int32)

    def decode_step(carry, pieces):
        grid_acc, grad_acc, source_acc = carry
        sources, targets = pieces
        gathered = jnp.take(mesh_out, sources, axis=0)
        pre = jnp.dot(gathered, w_decode, preferred_element_type=jnp.float32)
        message = jax.nn.silu(pre).astype(jnp.bfloat16)
        grid_acc = grid_acc.at[targets].add(message.astype(jnp.float32))
        edge_cot = jnp.take(grid_cotangent, targets, axis=0).astype(jnp.float32)
        d_pre = (edge_cot * silu_slope(pre)).astype(jnp.bfloat16)
        grad_acc = grad_acc + jnp.dot(gathered.T, d_pre, preferred_element_type=jnp.float32)
        source_acc = source_acc.at[sources].add(d_pre.astype(jnp.float32))
        return ((grid_acc, grad_acc, source_acc), None)
    start = (jnp.zeros((GRID, width), jnp.float32), jnp.zeros((width, width), jnp.float32), jnp.zeros((nodes, width), jnp.float32))
    pieces = (src_flat.reshape(DEVICES, per_dev), target.reshape(DEVICES, per_dev))
    (grid_acc, grad_decode, source_acc), _ = lax.scan(decode_step, start, pieces)
    grid_out = grid_acc.astype(jnp.bfloat16)
    per_source = source_acc.astype(jnp.bfloat16)
    d_out = jnp.dot(per_source, w_decode.T, preferred_element_type=jnp.float32)
    d_node = (d_out * silu_slope(npre)).astype(jnp.bfloat16)
    grad_node = jnp.dot(agg.T, d_node, preferred_element_type=jnp.float32)
    d_coarse = jnp.dot(onehot.T, d_node, preferred_element_type=jnp.float32)
    grad_coarse = jnp.dot(coarse_in.astype(jnp.float32).T, d_coarse * silu_slope(cpre), precision=lax.Precision.HIGHEST)
    d_agg = jnp.dot(d_node, w_node.T, preferred_element_type=jnp.float32)
    d_edges = (d_agg[None] * silu_slope(edges_pre)).astype(jnp.bfloat16)
    grad_source = jnp.dot(beside.T, d_edges.reshape(6 * nodes, width), preferred_element_type=jnp.float32)
    d_sum = lax.optimization_barrier(jnp.sum(d_edges.astype(jnp.float32), 0)).astype(jnp.bfloat16)
    grad_target = jnp.dot(latent.T, d_sum, preferred_element_type=jnp.float32)
    grads = jnp.stack([grad_source, grad_target, grad_node, grad_coarse, grad_decode])
    norm = jnp.sqrt(jnp.sum(grads * grads))
    clipped = (grads / (norm + 1e-06)).reshape(5, width * width)
    return (mesh_out.reshape(height, breadth, width), grid_out, clipped)
```

```python
import jax
import jax.numpy as jnp
from jax import lax
from jax.sharding import PartitionSpec as P

CAP = 3
AXES = ("lat", "lon")
F32 = jnp.float32
BF16 = jnp.bfloat16


def silu_slope(value):
    sig = jax.nn.sigmoid(value)
    return sig * (1.0 + value * (1.0 - sig))


def mm(left, right):
    return jnp.dot(left, right, preferred_element_type=F32)


def mm_t(left, right):
    return lax.dot_general(left, right, (((0,), (0,)), ((), ())), preferred_element_type=F32)


def mm_nt(left, right):
    return lax.dot_general(left, right, (((1,), (1,)), ((), ())), preferred_element_type=F32)


def split_counts(counts):
    high = jnp.floor(counts * (1.0 / 256.0)) * 256.0
    return high.astype(BF16), (counts - high).astype(BF16)


def split_float(value):
    high = value.astype(BF16)
    return high, (value - high.astype(F32)).astype(BF16)


def shift(value, axis, step):
    count = lax.axis_size(axis)
    return lax.ppermute(value, axis, [(i, (i + step) % count) for i in range(count)])


def packed_edges(edge_source, edge_target, edge_owner, grid_rows, nodes):
    lon_pos = lax.axis_index("lon")
    lon_count = lax.axis_size("lon")
    blocks = edge_owner.shape[0]
    block_len = edge_source.shape[0] // blocks
    side = (edge_owner[:, 0] - lon_pos + lon_count) % lon_count
    to_left = (side == lon_count - 1).astype(jnp.int32)
    to_right = (side == 1).astype(jnp.int32)
    tri = (jnp.arange(blocks)[:, None] > jnp.arange(blocks)[None, :]).astype(jnp.int32)
    left_rank = jnp.sum(tri * to_left[None, :], 1)
    right_rank = jnp.sum(tri * to_right[None, :], 1)
    place = jnp.where(to_left == 1, left_rank, jnp.where(to_right == 1, CAP + right_rank, -1))
    placing = jnp.arange(2 * CAP, dtype=jnp.int32)[:, None] == place[None, :]
    sources = edge_source.reshape(blocks, block_len)
    targets = edge_target.reshape(blocks, block_len)
    code = sources * (grid_rows + 1) + targets + 1
    packed = jnp.sum(jnp.where(placing[:, :, None], code[None], 0), 1).reshape(2, CAP * block_len)
    own_target = jnp.where((side == 0)[:, None], targets, -1).reshape(-1)
    return own_target, packed


def local(
    mesh_latent,
    grid_cotangent,
    w_source,
    w_target,
    w_node,
    w_coarse,
    w_decode,
    neighbour_codes,
    coarse_ids,
    edge_source,
    edge_target,
    edge_owner,
):
    height, breadth, width = mesh_latent.shape
    nodes = height * breadth
    grid_rows = grid_cotangent.shape[0]
    lat_pos, lon_pos = lax.axis_index("lat"), lax.axis_index("lon")
    lat_count, lon_count = lax.axis_size("lat"), lax.axis_size("lon")
    latent = mesh_latent.reshape(nodes, width)
    ids = coarse_ids.reshape(nodes)
    everyone = lax.all_gather(latent, AXES, axis=0, tiled=True)
    all_ids = lax.all_gather(ids, AXES, axis=0, tiled=True)

    own_target, packed = packed_edges(edge_source, edge_target, edge_owner, grid_rows, nodes)
    from_right = shift(packed[0], "lon", -1)
    from_left = shift(packed[1], "lon", 1)
    foreign = jnp.concatenate([from_left, from_right])
    offsets = jnp.repeat(jnp.array([1, 2], jnp.int32) * nodes, from_left.shape[0])
    every_target = jnp.concatenate([own_target, foreign % (grid_rows + 1) - 1])
    every_source = jnp.concatenate([edge_source, foreign // (grid_rows + 1) + offsets])
    target_hot = (jnp.arange(grid_rows, dtype=jnp.int32)[:, None] == every_target[None]).astype(BF16)
    source_hot = (every_source[:, None] == jnp.arange(3 * nodes, dtype=jnp.int32)[None]).astype(BF16)
    counts = mm(target_hot, source_hot)
    count_high, count_low = split_counts(counts)
    cot_sums = mm_t(count_high, grid_cotangent) + mm_t(count_low, grid_cotangent)
    back = cot_sums[nodes:].astype(BF16)
    cot_sum = (
        cot_sums[:nodes]
        + shift(back[:nodes], "lon", -1).astype(F32)
        + shift(back[nodes:], "lon", 1).astype(F32)
    )

    rows = lat_pos * height + jnp.arange(height, dtype=jnp.int32)[None, :, None] + neighbour_codes // 3 - 1
    cols = lon_pos * breadth + jnp.arange(breadth, dtype=jnp.int32)[None, None, :] + neighbour_codes % 3 - 1
    inside = (rows >= 0) & (rows < lat_count * height)
    cols = (cols + lon_count * breadth) % (lon_count * breadth)
    where_idx = ((rows // height) * lon_count + cols // breadth) * nodes + (rows % height) * breadth + cols % breadth
    where_idx = jnp.where(inside, where_idx, -1).reshape(-1)
    positions = jnp.arange(everyone.shape[0], dtype=jnp.int32)
    beside = mm((where_idx[:, None] == positions[None]).astype(BF16), everyone).astype(BF16)
    toward = mm(latent, w_target)
    edges_pre = mm(beside, w_source).reshape(6, nodes, width) + toward[None]
    agg = jnp.sum(jax.nn.silu(edges_pre), 0).astype(BF16)

    same = (ids[:, None] == all_ids[None]).astype(BF16)
    pooled = mm(same, everyone)
    count = jnp.sum(same.astype(F32), 1)
    coarse_in = (pooled * lax.rsqrt(count)[:, None]).astype(BF16)
    cpre = mm(coarse_in, w_coarse)
    coarse_out = jax.nn.silu(cpre).astype(BF16)
    npre = mm(agg, w_node) + coarse_out.astype(F32)
    mesh_out = (latent.astype(F32) + jax.nn.silu(npre)).astype(BF16)

    pre = mm(mesh_out, w_decode)
    message = jax.nn.silu(pre).astype(BF16)
    messages = jnp.concatenate([message, shift(message, "lon", 1), shift(message, "lon", -1)], 0)
    grid_out = (mm(count_high, messages) + mm(count_low, messages)).astype(BF16)

    d_pre = cot_sum * silu_slope(pre)
    d_high, d_low = split_float(d_pre)
    grad_decode = mm_t(mesh_out, d_high) + mm_t(mesh_out, d_low)
    d_out = mm_nt(d_high, w_decode)
    d_node = (d_out * silu_slope(npre)).astype(BF16)
    grad_node = mm_t(agg, d_node)
    c_high, c_low = split_float(d_node.astype(F32) * silu_slope(cpre))
    grad_coarse = mm_t(coarse_in, c_high) + mm_t(coarse_in, c_low)
    d_agg = mm_nt(d_node, w_node)
    d_edges = (d_agg[None] * silu_slope(edges_pre)).astype(BF16)
    grad_source = mm_t(beside, d_edges.reshape(6 * nodes, width))
    d_sum = jnp.sum(d_edges.astype(F32), 0).astype(BF16)
    grad_target = mm_t(latent, d_sum)
    stacked = jnp.stack([grad_source, grad_target, grad_node, grad_coarse, grad_decode]).reshape(
        5, width * width
    )
    share = lax.psum_scatter(stacked, AXES, scatter_dimension=1, tiled=True)
    norm = jnp.sqrt(lax.psum(jnp.sum(share * share), AXES))
    clipped = share / (norm + 1e-06)
    return (mesh_out.reshape(height, breadth, width), grid_out, clipped)


def solution(mesh):
    in_specs = (
        P("lat", "lon", None),
        P(("lat", "lon"), None),
        P(),
        P(),
        P(),
        P(),
        P(),
        P(None, "lat", "lon"),
        P("lat", "lon", None),
        P(("lat", "lon")),
        P(("lat", "lon")),
        P(("lat", "lon"), None),
    )
    out_specs = (P("lat", "lon", None), P(("lat", "lon"), None), P(None, ("lat", "lon")))
    return jax.shard_map(local, mesh=mesh, in_specs=in_specs, out_specs=out_specs, check_vma=False)
```

```python
import functools
import math

import jax
import jax.numpy as jnp
from jax import lax
from jax.experimental import pallas as pl
from jax.experimental.pallas import tpu as pltpu
from jax.sharding import PartitionSpec as P

CAP = 3
F32 = jnp.float32
BF16 = jnp.bfloat16


def silu_slope(value):
    sig = jax.nn.sigmoid(value)
    return sig * (1.0 + value * (1.0 - sig))


def mm(left, right):
    return jnp.dot(left, right, preferred_element_type=F32)


def mm_t(left, right):
    return lax.dot_general(left, right, (((0,), (0,)), ((), ())), preferred_element_type=F32)


def mm_nt(left, right):
    return lax.dot_general(left, right, (((1,), (1,)), ((), ())), preferred_element_type=F32)


def split_counts(counts):
    high = jnp.floor(counts * (1.0 / 256.0)) * 256.0
    return high.astype(BF16), (counts - high).astype(BF16)


def split_float(value):
    high = value.astype(BF16)
    return high, (value - high.astype(F32)).astype(BF16)


def shift(value, axis, step):
    count = lax.axis_size(axis)
    return lax.ppermute(value, axis, [(i, (i + step) % count) for i in range(count)])


def packed_edges(edge_source, edge_target, edge_owner, grid_rows, nodes):
    lon_pos = lax.axis_index("lon")
    lon_count = lax.axis_size("lon")
    blocks = edge_owner.shape[0]
    block_len = edge_source.shape[0] // blocks
    side = (edge_owner[:, 0] - lon_pos + lon_count) % lon_count
    to_left = (side == lon_count - 1).astype(jnp.int32)
    to_right = (side == 1).astype(jnp.int32)
    tri = (jnp.arange(blocks)[:, None] > jnp.arange(blocks)[None, :]).astype(jnp.int32)
    left_rank = jnp.sum(tri * to_left[None, :], 1)
    right_rank = jnp.sum(tri * to_right[None, :], 1)
    place = jnp.where(to_left == 1, left_rank, jnp.where(to_right == 1, CAP + right_rank, -1))
    placing = jnp.arange(2 * CAP, dtype=jnp.int32)[:, None] == place[None, :]
    sources = edge_source.reshape(blocks, block_len)
    targets = edge_target.reshape(blocks, block_len)
    code = sources * (grid_rows + 1) + targets + 1
    packed = jnp.sum(jnp.where(placing[:, :, None], code[None], 0), 1).reshape(2, CAP * block_len)
    own_target = jnp.where((side == 0)[:, None], targets, -1).reshape(-1)
    return own_target, packed


MESH = pl.DeviceIdType.MESH


class Place:
    def __init__(self, sizes):
        self.Z, self.Y, self.X, self.C = sizes
        self.L = self.Y * self.X * self.C
        self.lat, self.lon = lax.axis_index("lat"), lax.axis_index("lon")
        self.z, self.c = self.lat, lax.rem(self.lon, self.C)
        self.x = lax.rem(self.lon // self.C, self.X)
        self.y = self.lon // (self.C * self.X)

    def at(self, y=None, x=None, c=None):
        y, x, c = (old if new is None else new for new, old in ((y, self.y), (x, self.x), (c, self.c)))
        return (self.lat, (y * self.X + x) * self.C + c)

    def meet(self):
        barrier = pltpu.get_barrier_semaphore()
        for step in range(1, self.Z):
            peer = (lax.rem(self.z + step, self.Z), self.lon)
            pl.semaphore_signal(barrier, inc=1, device_id=peer, device_id_type=MESH)
        for step in range(1, self.L):
            peer = (self.lat, lax.rem(self.lon + step, self.L))
            pl.semaphore_signal(barrier, inc=1, device_id=peer, device_id_type=MESH)
        pl.semaphore_wait(barrier, self.Z - 1 + self.L - 1)


def send(src, dst, sems, slot, peer):
    copy = pltpu.make_async_remote_copy(
        src_ref=src, dst_ref=dst, send_sem=sems.at[0, slot], recv_sem=sems.at[1, slot],
        device_id=peer, device_id_type=MESH,
    )
    copy.start()
    return copy


def gather_kernel(sizes, lat_ref, id_ref, edge_ref, all_ref, all_id_ref, left_ref, right_ref, sems):
    p = Place(sizes)
    Z, Y, X, C, z, y, x, c = p.Z, p.Y, p.X, p.C, p.z, p.y, p.x, p.c
    half = lat_ref.shape[0] // 2
    low, high = pl.ds(0, half), pl.ds(half, half)
    used = [0]
    copies = []

    def go(src, dst, peer):
        copy = send(src, dst, sems, used[0], peer)
        used[0] += 1
        copies.append(copy)
        return copy

    all_ref[z, y, x, c] = lat_ref[...]
    all_id_ref[z, y, x, c] = id_ref[...]
    p.meet()
    first = []
    for step in range(1, Z):
        peer = (lax.rem(z + step, Z), p.lon)
        first.append([
            go(lat_ref, all_ref.at[z, y, x, c], peer),
            go(id_ref, all_id_ref.at[z, y, x, c], peer),
        ])
    edges = [
        go(edge_ref.at[0], right_ref, (p.lat, lax.rem(p.lon + p.L - 1, p.L))),
        go(edge_ref.at[1], left_ref, (p.lat, lax.rem(p.lon + 1, p.L))),
    ]
    second = []
    for step in range(Z):
        line = lax.rem(z + Z - step, Z)
        if step:
            for copy in first[step - 1]:
                copy.wait_recv()
        mine = []
        block = all_ref.at[line, y, x, c]
        src_low = block.at[low] if step else lat_ref.at[low]
        src_high = block.at[high] if step else lat_ref.at[high]
        src_id = all_id_ref.at[line, y, x, c] if step else id_ref
        for off in range(1, X):
            peer = p.at(x=lax.rem(x + off, X))
            mine.append(go(src_low, block.at[low], peer))
            mine.append(go(src_id, all_id_ref.at[line, y, x, c], peer))
        for off in range(1, Y):
            mine.append(go(src_high, block.at[high], p.at(y=lax.rem(y + off, Y))))
        second.append(mine)
    third = []
    for step in range(Z):
        line = lax.rem(z + Z - step, Z)
        for copy in second[step]:
            copy.wait_recv()
        mine = []
        for off in range(1, Y):
            peer = p.at(y=lax.rem(y + off, Y))
            part = all_ref.at[line, y, :, c, low]
            mine.append(go(part, part, peer))
            part = all_id_ref.at[line, y, :, c]
            mine.append(go(part, part, peer))
        for off in range(1, X):
            part = all_ref.at[line, :, x, c, high]
            mine.append(go(part, part, p.at(x=lax.rem(x + off, X))))
        third.append(mine)
    fourth = []
    for step in range(Z):
        line = lax.rem(z + Z - step, Z)
        for copy in third[step]:
            copy.wait_recv()
        for off in range(1, C):
            peer = p.at(c=lax.rem(c + off, C))
            part = all_ref.at[line, :, :, c]
            fourth.append(go(part, part, peer))
            part = all_id_ref.at[line, :, :, c]
            fourth.append(go(part, part, peer))
    for copy in edges + fourth:
        copy.wait_recv()
    for copy in copies:
        copy.wait_send()


def gather_all(sizes, latent, ids, packed):
    Z, Y, X, C = sizes
    nodes, width = latent.shape
    sends = (Z - 1) * 2 + 2 + Z * (3 * (X - 1) + 3 * (Y - 1) + 2 * (C - 1))
    vmem = pl.BlockSpec(memory_space=pltpu.VMEM)
    row = packed.shape[1:]
    return pl.pallas_call(
        functools.partial(gather_kernel, sizes),
        out_shape=(
            jax.ShapeDtypeStruct((Z, Y, X, C, nodes, width), latent.dtype),
            jax.ShapeDtypeStruct((Z, Y, X, C, *ids.shape), ids.dtype),
            jax.ShapeDtypeStruct(row, packed.dtype),
            jax.ShapeDtypeStruct(row, packed.dtype),
        ),
        in_specs=[vmem] * 3,
        out_specs=(vmem,) * 4,
        scratch_shapes=[pltpu.SemaphoreType.DMA((2, sends))],
        compiler_params=pltpu.CompilerParams(collective_id=0, has_side_effects=True),
        name="gather_all",
    )(latent, ids, packed)


def reduce_kernel(sizes, *refs):
    grads, refs = refs[:5], refs[5:]
    out_ref, s1, r1, acc1, s2, r2, acc2, s3, r3, acc3, s4, r4, sq, zq, lq = refs[:15]
    sem1, sem2, sem3, sem4, zsem, lsem = refs[15:]
    p = Place(sizes)
    Z, Y, X, C, z, y, x, c = p.Z, p.Y, p.X, p.C, p.z, p.y, p.x, p.c
    many = len(grads)
    w2 = out_ref.shape[-1] // 2
    halves = (pl.ds(0, w2), pl.ds(w2, w2))
    p.meet()
    copies = []

    def go(src, dst, sems, slot, peer):
        copy = send(src, dst, sems, slot, peer)
        copies.append(copy)
        return copy

    first = []
    for m in range(many):
        mine = []
        for off in range(1, C):
            there = lax.rem(c + off, C)
            k = m * (C - 1) + off - 1
            s1[k] = grads[m][:, :, :, there].astype(BF16)
            mine.append((k, go(s1.at[k], r1.at[k], sem1, k, p.at(c=there))))
        first.append(mine)
    second = []
    for m in range(many):
        total = grads[m][:, :, :, c]
        for k, copy in first[m]:
            copy.wait_recv()
            total = total + r1[k].astype(F32)
        acc1[m] = total
        mine = ([], [])
        for off in range(1, X):
            there = lax.rem(x + off, X)
            k = m * (X - 1) + off - 1
            s2[0][k] = acc1[m, :, :, there, :, halves[0]].astype(BF16)
            mine[0].append((k, go(s2[0].at[k], r2[0].at[k], sem2[0], k, p.at(x=there))))
        for off in range(1, Y):
            there = lax.rem(y + off, Y)
            k = m * (Y - 1) + off - 1
            s2[1][k] = acc1[m, :, there, :, :, halves[1]].astype(BF16)
            mine[1].append((k, go(s2[1].at[k], r2[1].at[k], sem2[1], k, p.at(y=there))))
        second.append(mine)
    third = []
    for m in range(many):
        mine = ([], [])
        total = acc1[m, :, :, x, :, halves[0]]
        for k, copy in second[m][0]:
            copy.wait_recv()
            total = total + r2[0][k].astype(F32)
        acc2[0][m] = total
        for off in range(1, Y):
            there = lax.rem(y + off, Y)
            k = m * (Y - 1) + off - 1
            s3[0][k] = acc2[0][m, :, there].astype(BF16)
            mine[0].append((k, go(s3[0].at[k], r3[0].at[k], sem3[0], k, p.at(y=there))))
        total = acc1[m, :, y, :, :, halves[1]]
        for k, copy in second[m][1]:
            copy.wait_recv()
            total = total + r2[1][k].astype(F32)
        acc2[1][m] = total
        for off in range(1, X):
            there = lax.rem(x + off, X)
            k = m * (X - 1) + off - 1
            s3[1][k] = acc2[1][m, :, there].astype(BF16)
            mine[1].append((k, go(s3[1].at[k], r3[1].at[k], sem3[1], k, p.at(x=there))))
        third.append(mine)
    fourth = []
    for m in range(many):
        for side, own in ((0, y), (1, x)):
            total = acc2[side][m, :, own]
            for k, copy in third[m][side]:
                copy.wait_recv()
                total = total + r3[side][k].astype(F32)
            acc3[m, :, :, halves[side]] = total
        mine = []
        for off in range(1, Z):
            there = lax.rem(z + off, Z)
            k = m * (Z - 1) + off - 1
            s4[k] = acc3[m, there].astype(BF16)
            mine.append((k, go(s4.at[k], r4.at[k], sem4, k, (there, p.lon))))
        fourth.append(mine)
    square = jnp.zeros(out_ref.shape[1:], F32)
    for m in range(many):
        total = acc3[m, z]
        for k, copy in fourth[m]:
            copy.wait_recv()
            total = total + r4[k].astype(F32)
        out_ref[m] = total
        square = square + total * total
    sq[0] = jnp.broadcast_to(jnp.sum(square, keepdims=True), sq.shape[1:])
    mine = []
    for off in range(1, Z):
        mine.append(go(sq.at[0], zq.at[off - 1], zsem, off - 1, (lax.rem(z + off, Z), p.lon)))
    whole = sq[0]
    for off, copy in enumerate(mine):
        copy.wait_recv()
        whole = whole + zq[off]
    sq[1] = whole
    mine = []
    for off in range(1, p.L):
        mine.append(go(sq.at[1], lq.at[off - 1], lsem, off - 1, (p.lat, lax.rem(p.lon + off, p.L))))
    for off, copy in enumerate(mine):
        copy.wait_recv()
        whole = whole + lq[off]
    norm = jnp.sqrt(whole[0:1, 0:1]) + 1e-06
    for m in range(many):
        out_ref[m] = out_ref[m] / norm
    for copy in copies:
        copy.wait_send()


def reduce_all(sizes, grads):
    Z, Y, X, C = sizes
    L = Y * X * C
    many = len(grads)
    wide, width = grads[0].shape
    R = wide // (Z * L)
    w2 = width // 2
    vmem = pl.BlockSpec(memory_space=pltpu.VMEM)

    def buf(dtype, *dims):
        return pltpu.VMEM(dims, dtype)

    def two(count):
        return [pltpu.SemaphoreType.DMA((2, n)) for n in count]

    nx, ny, nz, nc = many * (X - 1), many * (Y - 1), many * (Z - 1), many * (C - 1)
    second = [buf(BF16, nx, Z, Y, R, w2), buf(BF16, ny, Z, X, R, w2)]
    third = [buf(BF16, ny, Z, R, w2), buf(BF16, nx, Z, R, w2)]
    return pl.pallas_call(
        functools.partial(reduce_kernel, sizes),
        out_shape=jax.ShapeDtypeStruct((many, R, width), F32),
        in_specs=[vmem] * many,
        out_specs=vmem,
        scratch_shapes=[
            buf(BF16, nc, Z, Y, X, R, width), buf(BF16, nc, Z, Y, X, R, width),
            buf(F32, many, Z, Y, X, R, width),
            second, second, [buf(F32, many, Z, Y, R, w2), buf(F32, many, Z, X, R, w2)],
            third, third, buf(F32, many, Z, R, width),
            buf(BF16, nz, R, width), buf(BF16, nz, R, width),
            buf(F32, 2, 8, 128), buf(F32, Z - 1, 8, 128), buf(F32, L - 1, 8, 128),
            *two([nc]), two([nx, ny]), two([ny, nx]), *two([nz, Z - 1, L - 1]),
        ],
        compiler_params=pltpu.CompilerParams(
            collective_id=1, has_side_effects=True, vmem_limit_bytes=60 * 1024 * 1024
        ),
        name="reduce_all",
    )(*[grad.reshape(Z, Y, X, C, R, width) for grad in grads])


def lon_parts(lat_count, lon_count):
    chips = lon_count // 2
    x = next(d for d in range(math.isqrt(chips), 0, -1) if chips % d == 0)
    return lat_count, chips // x, x, 2


def local(
    mesh_latent,
    grid_cotangent,
    w_source,
    w_target,
    w_node,
    w_coarse,
    w_decode,
    neighbour_codes,
    coarse_ids,
    edge_source,
    edge_target,
    edge_owner,
):
    height, breadth, width = mesh_latent.shape
    nodes = height * breadth
    grid_rows = grid_cotangent.shape[0]
    lat_pos, lon_pos = lax.axis_index("lat"), lax.axis_index("lon")
    lat_count, lon_count = lax.axis_size("lat"), lax.axis_size("lon")
    latent = mesh_latent.reshape(nodes, width)
    ids = coarse_ids.reshape(nodes)
    sizes = lon_parts(lat_count, lon_count)

    own_target, packed = packed_edges(edge_source, edge_target, edge_owner, grid_rows, nodes)
    everyone, all_ids, from_left, from_right = gather_all(sizes, latent, ids[None], packed[:, None])
    everyone, all_ids = everyone.reshape(-1, width), all_ids.reshape(-1)
    from_left, from_right = from_left[0], from_right[0]
    foreign = jnp.concatenate([from_left, from_right])
    offsets = jnp.repeat(jnp.array([1, 2], jnp.int32) * nodes, from_left.shape[0])
    every_target = jnp.concatenate([own_target, foreign % (grid_rows + 1) - 1])
    every_source = jnp.concatenate([edge_source, foreign // (grid_rows + 1) + offsets])
    target_hot = (jnp.arange(grid_rows, dtype=jnp.int32)[:, None] == every_target[None]).astype(BF16)
    source_hot = (every_source[:, None] == jnp.arange(3 * nodes, dtype=jnp.int32)[None]).astype(BF16)
    counts = mm(target_hot, source_hot)
    count_high, count_low = split_counts(counts)
    cot_sums = mm_t(count_high, grid_cotangent) + mm_t(count_low, grid_cotangent)
    back = cot_sums[nodes:].astype(BF16)
    cot_sum = (
        cot_sums[:nodes]
        + shift(back[:nodes], "lon", -1).astype(F32)
        + shift(back[nodes:], "lon", 1).astype(F32)
    )

    rows = lat_pos * height + jnp.arange(height, dtype=jnp.int32)[None, :, None] + neighbour_codes // 3 - 1
    cols = lon_pos * breadth + jnp.arange(breadth, dtype=jnp.int32)[None, None, :] + neighbour_codes % 3 - 1
    inside = (rows >= 0) & (rows < lat_count * height)
    cols = (cols + lon_count * breadth) % (lon_count * breadth)
    where_idx = ((rows // height) * lon_count + cols // breadth) * nodes + (rows % height) * breadth + cols % breadth
    where_idx = jnp.where(inside, where_idx, -1).reshape(-1)
    positions = jnp.arange(everyone.shape[0], dtype=jnp.int32)
    beside = mm((where_idx[:, None] == positions[None]).astype(BF16), everyone).astype(BF16)
    toward = mm(latent, w_target)
    edges_pre = mm(beside, w_source).reshape(6, nodes, width) + toward[None]
    agg = jnp.sum(jax.nn.silu(edges_pre), 0).astype(BF16)

    same = (ids[:, None] == all_ids[None]).astype(BF16)
    pooled = mm(same, everyone)
    count = jnp.sum(same.astype(F32), 1)
    coarse_in = (pooled * lax.rsqrt(count)[:, None]).astype(BF16)
    cpre = mm(coarse_in, w_coarse)
    coarse_out = jax.nn.silu(cpre).astype(BF16)
    npre = mm(agg, w_node) + coarse_out.astype(F32)
    mesh_out = (latent.astype(F32) + jax.nn.silu(npre)).astype(BF16)

    pre = mm(mesh_out, w_decode)
    message = jax.nn.silu(pre).astype(BF16)
    messages = jnp.concatenate([message, shift(message, "lon", 1), shift(message, "lon", -1)], 0)
    grid_out = (mm(count_high, messages) + mm(count_low, messages)).astype(BF16)

    d_pre = cot_sum * silu_slope(pre)
    d_high, d_low = split_float(d_pre)
    grad_decode = mm_t(mesh_out, d_high) + mm_t(mesh_out, d_low)
    d_out = mm_nt(d_high, w_decode)
    d_node = (d_out * silu_slope(npre)).astype(BF16)
    grad_node = mm_t(agg, d_node)
    c_high, c_low = split_float(d_node.astype(F32) * silu_slope(cpre))
    grad_coarse = mm_t(coarse_in, c_high) + mm_t(coarse_in, c_low)
    d_agg = mm_nt(d_node, w_node)
    d_edges = (d_agg[None] * silu_slope(edges_pre)).astype(BF16)
    grad_source = mm_t(beside, d_edges.reshape(6 * nodes, width))
    d_sum = jnp.sum(d_edges.astype(F32), 0).astype(BF16)
    grad_target = mm_t(latent, d_sum)
    clipped = reduce_all(sizes, (grad_source, grad_target, grad_node, grad_coarse, grad_decode))
    clipped = clipped.reshape(clipped.shape[0], -1)
    return (mesh_out.reshape(height, breadth, width), grid_out, clipped)


def solution(mesh):
    in_specs = (
        P("lat", "lon", None),
        P(("lat", "lon"), None),
        P(),
        P(),
        P(),
        P(),
        P(),
        P(None, "lat", "lon"),
        P("lat", "lon", None),
        P(("lat", "lon")),
        P(("lat", "lon")),
        P(("lat", "lon"), None),
    )
    out_specs = (P("lat", "lon", None), P(("lat", "lon"), None), P(None, ("lat", "lon")))
    return jax.shard_map(local, mesh=mesh, in_specs=in_specs, out_specs=out_specs, check_vma=False)
```

```python
import functools
import math

import jax
import jax.numpy as jnp
from jax import lax
from jax.experimental import pallas as pl
from jax.experimental.pallas import tpu as pltpu
from jax.sharding import PartitionSpec as P

CAP = 3
F32 = jnp.float32
BF16 = jnp.bfloat16


def silu_slope(value):
    sig = jax.nn.sigmoid(value)
    return sig * (1.0 + value * (1.0 - sig))


def mm(left, right):
    return jnp.dot(left, right, preferred_element_type=F32)


def mm_t(left, right):
    return lax.dot_general(left, right, (((0,), (0,)), ((), ())), preferred_element_type=F32)


def mm_nt(left, right):
    return lax.dot_general(left, right, (((1,), (1,)), ((), ())), preferred_element_type=F32)


def split_float(value):
    high = value.astype(BF16)
    return high, (value - high.astype(F32)).astype(BF16)


MESH = pl.DeviceIdType.MESH


class Place:
    def __init__(self, sizes):
        self.Z, self.Y, self.X, self.C = sizes
        self.L = self.Y * self.X * self.C
        self.lat, self.lon = lax.axis_index("lat"), lax.axis_index("lon")
        self.z, self.c = self.lat, lax.rem(self.lon, self.C)
        self.x = lax.rem(self.lon // self.C, self.X)
        self.y = self.lon // (self.C * self.X)

    def at(self, y=None, x=None, c=None):
        y, x, c = (old if new is None else new for new, old in ((y, self.y), (x, self.x), (c, self.c)))
        return (self.lat, (y * self.X + x) * self.C + c)

    def meet(self):
        barrier = pltpu.get_barrier_semaphore()
        for step in range(1, self.Z):
            peer = (lax.rem(self.z + step, self.Z), self.lon)
            pl.semaphore_signal(barrier, inc=1, device_id=peer, device_id_type=MESH)
        for step in range(1, self.L):
            peer = (self.lat, lax.rem(self.lon + step, self.L))
            pl.semaphore_signal(barrier, inc=1, device_id=peer, device_id_type=MESH)
        pl.semaphore_wait(barrier, self.Z - 1 + self.L - 1)


def send(src, dst, sems, slot, peer):
    copy = pltpu.make_async_remote_copy(
        src_ref=src, dst_ref=dst, send_sem=sems.at[0, slot], recv_sem=sems.at[1, slot],
        device_id=peer, device_id_type=MESH,
    )
    copy.start()
    return copy


def iota(shape, dim):
    return lax.broadcasted_iota(jnp.int32, shape, dim)


def step_kernel(sizes, *refs):
    (lat_ref, cot_ref, ws_ref, wt_ref, wn_ref, wc_ref, wd_ref, where_ref, id_ref, idcol_ref, src_ref, tgt_ref,
     owner_ref) = refs[:13]
    mesh_ref, grid_ref, out_ref = refs[13:16]
    (all_ref, all_id, near, pack, erow, counts, cnt_high, cnt_low, back, backs, msgs, grad, s1, r1, acc1, s2, r2, acc2,
     s3, r3, acc3, s4, r4, sq, zq, lq) = refs[16:42]
    gsem, esem, sem1, sem2, sem3, sem4, zsem, lsem = refs[42:]
    p = Place(sizes)
    Z, Y, X, C, z, y, x, c = p.Z, p.Y, p.X, p.C, p.z, p.y, p.x, p.c
    nodes, width = lat_ref.shape
    grid_rows = cot_ref.shape[0]
    blocks, block_len = src_ref.shape
    lanes = counts.shape[1]
    to_left = (p.lat, lax.rem(p.lon + p.L - 1, p.L))
    to_right = (p.lat, lax.rem(p.lon + 1, p.L))
    many = out_ref.shape[0]
    R = out_ref.shape[1]
    w2 = width // 2
    halves = (pl.ds(0, w2), pl.ds(w2, w2))
    half = nodes // 2
    low, high = pl.ds(0, half), pl.ds(half, half)
    copies = []
    used = [0]

    def go(src, dst, sems, slot, peer):
        copy = send(src, dst, sems, slot, peer)
        copies.append(copy)
        return copy

    def pass_on(src, dst, peer):
        used[0] += 1
        return go(src, dst, gsem, used[0] - 1, peer)

    all_ref[z, y, x, c] = lat_ref[...]
    all_id[z, y, x, c] = id_ref[...]
    owner = owner_ref[...]
    is_left = (owner == lax.rem(p.lon + p.L - 1, p.L)).astype(jnp.int32)
    is_right = (owner == lax.rem(p.lon + 1, p.L)).astype(jnp.int32)
    sub, lane = iota((blocks, blocks), 0), iota((blocks, blocks), 1)

    def ranks(column):
        row = jnp.sum(jnp.where(sub == lane, jnp.broadcast_to(column, sub.shape), 0), 0, keepdims=True)
        return jnp.sum(jnp.where(lane < sub, jnp.broadcast_to(row, sub.shape), 0), 1, keepdims=True)

    place = jnp.where(is_left == 1, ranks(is_left), jnp.where(is_right == 1, CAP + ranks(is_right), -1))
    wide_place = jnp.broadcast_to(place, (blocks, block_len))
    for r in range(2 * CAP):
        mine = wide_place == r
        side, row = divmod(r, CAP)
        pack[side, 0, row:row + 1] = jnp.sum(jnp.where(mine, src_ref[...], 0), 0, keepdims=True)
        pack[side, 1, row:row + 1] = jnp.sum(jnp.where(mine, tgt_ref[...] + 1, 0), 0, keepdims=True) - 1
    p.meet()
    first = []
    for step in range(1, Z):
        peer = (lax.rem(z + step, Z), p.lon)
        first.append([
            pass_on(lat_ref, all_ref.at[z, y, x, c], peer),
            pass_on(id_ref, all_id.at[z, y, x, c], peer),
        ])
    edges = [go(pack.at[0], pack.at[3], esem, 0, to_left), go(pack.at[1], pack.at[2], esem, 1, to_right)]
    second, third, fourth = [], [], []

    def hop_two(step):
        line = lax.rem(z + Z - step, Z)
        if step:
            for copy in first[step - 1]:
                copy.wait_recv()
        mine = []
        block = all_ref.at[line, y, x, c]
        src_low = block.at[low] if step else lat_ref.at[low]
        src_high = block.at[high] if step else lat_ref.at[high]
        src_id = all_id.at[line, y, x, c] if step else id_ref
        for off in range(1, X):
            peer = p.at(x=lax.rem(x + off, X))
            mine.append(pass_on(src_low, block.at[low], peer))
            mine.append(pass_on(src_id, all_id.at[line, y, x, c], peer))
        for off in range(1, Y):
            mine.append(pass_on(src_high, block.at[high], p.at(y=lax.rem(y + off, Y))))
        second.append(mine)

    def hop_three(step):
        line = lax.rem(z + Z - step, Z)
        for copy in second[step]:
            copy.wait_recv()
        mine = []
        for off in range(1, Y):
            peer = p.at(y=lax.rem(y + off, Y))
            part = all_ref.at[line, y, :, c, low]
            mine.append(pass_on(part, part, peer))
            part = all_id.at[line, y, :, c]
            mine.append(pass_on(part, part, peer))
        for off in range(1, X):
            part = all_ref.at[line, :, x, c, high]
            mine.append(pass_on(part, part, p.at(x=lax.rem(x + off, X))))
        third.append(mine)

    def hop_four(step):
        line = lax.rem(z + Z - step, Z)
        for copy in third[step]:
            copy.wait_recv()
        for off in range(1, C):
            peer = p.at(c=lax.rem(c + off, C))
            part = all_ref.at[line, :, :, c]
            fourth.append(pass_on(part, part, peer))
            part = all_id.at[line, :, :, c]
            fourth.append(pass_on(part, part, peer))

    stays = jnp.broadcast_to((owner == p.lon).astype(jnp.int32), (blocks, block_len))
    erow[0, 0:blocks] = src_ref[...]
    erow[1, 0:blocks] = jnp.where(stays == 1, tgt_ref[...], -1)
    pair = 2 if blocks % 2 == 0 else 1

    def count(start, stop):
        for b in range(start, stop, pair):
            upto = min(b + pair, stop)
            tgt = jnp.concatenate([jnp.broadcast_to(erow[1, r:r + 1], (grid_rows, block_len)) for r in range(b, upto)], 1)
            src = jnp.concatenate([jnp.broadcast_to(erow[0, r:r + 1], (lanes, block_len)) for r in range(b, upto)], 1)
            hot_t = jnp.where(tgt == iota(tgt.shape, 0), 1.0, 0.0).astype(BF16)
            hot_s = jnp.where(src == iota(src.shape, 0), 1.0, 0.0).astype(BF16)
            more = mm_nt(hot_t, hot_s)
            counts[...] = more if b == 0 else counts[...] + more

    hop_two(0)
    third_of = blocks // 3 // pair * pair
    count(0, third_of)
    for step in range(1, Z):
        hop_two(step)
    count(third_of, 2 * third_of)
    for step in range(Z):
        hop_three(step)
    count(2 * third_of, blocks)
    for copy in edges:
        copy.wait_recv()
    for side in range(2):
        erow[0, blocks + side * CAP:blocks + (side + 1) * CAP] = pack[2 + side, 0] + (side + 1) * nodes
        erow[1, blocks + side * CAP:blocks + (side + 1) * CAP] = pack[2 + side, 1]
    count(blocks, blocks + 2 * CAP)
    over = jnp.floor(counts[...] * (1.0 / 256.0)) * 256.0
    cnt_high[...] = over.astype(BF16)
    cnt_low[...] = (counts[...] - over).astype(BF16)
    cot_sums = mm_t(cnt_high[...], cot_ref[...]) + mm_t(cnt_low[...], cot_ref[...])
    backs[0] = cot_sums[nodes:2 * nodes].astype(BF16)
    backs[1] = cot_sums[2 * nodes:3 * nodes].astype(BF16)
    returns = [go(backs.at[0], back.at[0], esem, 2, to_left), go(backs.at[1], back.at[1], esem, 3, to_right)]
    for step in range(Z):
        hop_four(step)
    latent = lat_ref[...]
    toward = mm(latent, wt_ref[...])
    for copy in fourth:
        copy.wait_recv()

    for r in range(3):
        for q in range(3):
            lon = lax.rem(p.lon + q - 1 + p.L, p.L)
            line = lax.rem(z + r - 1 + Z, Z)
            block = all_ref[line, lon // (C * X), lax.rem(lon // C, X), lax.rem(lon, C)]
            near[(r * 3 + q) * nodes:(r * 3 + q + 1) * nodes] = block
    hot = jnp.broadcast_to(where_ref[...], (where_ref.shape[0], near.shape[0]))
    hot = jnp.where(hot == iota(hot.shape, 1), 1.0, 0.0).astype(BF16)
    beside = mm(hot, near[...]).astype(BF16)
    slots = beside.shape[0] // nodes
    edges_pre = mm(beside, ws_ref[...]).reshape(slots, nodes, width) + toward[None]
    agg = jnp.sum(edges_pre * jax.nn.sigmoid(edges_pre), 0).astype(BF16)

    pooled = jnp.zeros((nodes, width), F32)
    count_of = jnp.zeros((nodes, 1), F32)
    for line in range(Z):
        ids = jnp.sum(all_id[line].reshape(Y * X, C, C * nodes), 1)
        row = jnp.concatenate([ids[q:q + 1] for q in range(Y * X)], 1)
        wide = jnp.broadcast_to(row, (nodes, row.shape[1]))
        same = jnp.where(wide == jnp.broadcast_to(idcol_ref[...], wide.shape), 1.0, 0.0)
        count_of = count_of + jnp.sum(same, 1, keepdims=True)
        pooled = pooled + mm(same.astype(BF16), all_ref[line].reshape(p.L * nodes, width))
    coarse_in = (pooled * lax.rsqrt(count_of)).astype(BF16)
    cpre = mm(coarse_in, wc_ref[...])
    coarse_out = (cpre * jax.nn.sigmoid(cpre)).astype(BF16)
    npre = mm(agg, wn_ref[...]) + coarse_out.astype(F32)
    mesh_out = (latent.astype(F32) + npre * jax.nn.sigmoid(npre)).astype(BF16)
    mesh_ref[...] = mesh_out

    pre = mm(mesh_out, wd_ref[...])
    msgs[0:nodes] = (pre * jax.nn.sigmoid(pre)).astype(BF16)
    if lanes > 3 * nodes:
        msgs[3 * nodes:] = jnp.zeros((lanes - 3 * nodes, width), BF16)
    mine = msgs.at[pl.ds(0, nodes)]
    spoken = [
        go(mine, msgs.at[pl.ds(nodes, nodes)], esem, 4, to_right),
        go(mine, msgs.at[pl.ds(2 * nodes, nodes)], esem, 5, to_left),
    ]

    one, two, three, four = {}, {}, {}, {}

    def hop_core(m, value):
        if R % 8 == 0:
            grad[m] = value.reshape(Z, Y, X, C, R, width)
        else:
            for q in range(Z * p.L):
                spot = (q // p.L, q // (C * X) % Y, q // C % X, q % C)
                grad[(m, *spot)] = value[q * R:(q + 1) * R]
        one[m] = []
        for off in range(1, C):
            there = lax.rem(c + off, C)
            k = m * (C - 1) + off - 1
            s1[k] = grad[m, :, :, :, there].astype(BF16)
            one[m].append((k, go(s1.at[k], r1.at[k], sem1, k, p.at(c=there))))

    def hop_first(m):
        total = grad[m, :, :, :, c]
        for k, copy in one[m]:
            copy.wait_recv()
            total = total + r1[k].astype(F32)
        acc1[m] = total
        two[m] = ([], [])
        for off in range(1, X):
            there = lax.rem(x + off, X)
            k = m * (X - 1) + off - 1
            s2[0][k] = acc1[m, :, :, there, :, halves[0]].astype(BF16)
            two[m][0].append((k, go(s2[0].at[k], r2[0].at[k], sem2[0], k, p.at(x=there))))
        for off in range(1, Y):
            there = lax.rem(y + off, Y)
            k = m * (Y - 1) + off - 1
            s2[1][k] = acc1[m, :, there, :, :, halves[1]].astype(BF16)
            two[m][1].append((k, go(s2[1].at[k], r2[1].at[k], sem2[1], k, p.at(y=there))))

    def hop_other(m):
        three[m] = ([], [])
        total = acc1[m, :, :, x, :, halves[0]]
        for k, copy in two[m][0]:
            copy.wait_recv()
            total = total + r2[0][k].astype(F32)
        acc2[0][m] = total
        for off in range(1, Y):
            there = lax.rem(y + off, Y)
            k = m * (Y - 1) + off - 1
            s3[0][k] = acc2[0][m, :, there].astype(BF16)
            three[m][0].append((k, go(s3[0].at[k], r3[0].at[k], sem3[0], k, p.at(y=there))))
        total = acc1[m, :, y, :, :, halves[1]]
        for k, copy in two[m][1]:
            copy.wait_recv()
            total = total + r2[1][k].astype(F32)
        acc2[1][m] = total
        for off in range(1, X):
            there = lax.rem(x + off, X)
            k = m * (X - 1) + off - 1
            s3[1][k] = acc2[1][m, :, there].astype(BF16)
            three[m][1].append((k, go(s3[1].at[k], r3[1].at[k], sem3[1], k, p.at(x=there))))

    def hop_line(m):
        for side, own in ((0, y), (1, x)):
            total = acc2[side][m, :, own]
            for k, copy in three[m][side]:
                copy.wait_recv()
                total = total + r3[side][k].astype(F32)
            acc3[m, :, :, halves[side]] = total
        four[m] = []
        for off in range(1, Z):
            there = lax.rem(z + off, Z)
            k = m * (Z - 1) + off - 1
            s4[k] = acc3[m, there].astype(BF16)
            four[m].append((k, go(s4.at[k], r4.at[k], sem4, k, (there, p.lon))))

    for copy in returns:
        copy.wait_recv()
    cot_sum = cot_sums[:nodes] + back[0].astype(F32) + back[1].astype(F32)
    d_high, d_low = split_float(cot_sum * silu_slope(pre))
    hop_core(4, mm_t(mesh_out, d_high) + mm_t(mesh_out, d_low))
    d_node = (mm_nt(d_high, wd_ref[...]) * silu_slope(npre)).astype(BF16)
    hop_core(2, mm_t(agg, d_node))
    hop_first(4)
    c_high, c_low = split_float(d_node.astype(F32) * silu_slope(cpre))
    hop_core(3, mm_t(coarse_in, c_high) + mm_t(coarse_in, c_low))
    hop_first(2)
    d_edges = (mm_nt(d_node, wn_ref[...])[None] * silu_slope(edges_pre)).astype(BF16)
    d_sum = jnp.sum(d_edges.astype(F32), 0).astype(BF16)
    hop_core(1, mm_t(latent, d_sum))
    hop_first(3)
    hop_core(0, mm_t(beside, d_edges.reshape(slots * nodes, width)))
    hop_first(1)
    hop_first(0)
    order = (4, 2, 3, 1, 0)
    hop_other(order[0])
    for copy in spoken:
        copy.wait_recv()
    grid_ref[...] = (mm(cnt_high[...], msgs[...]) + mm(cnt_low[...], msgs[...])).astype(BF16)
    for m in order[1:]:
        hop_other(m)
    for m in order:
        hop_line(m)
    square = jnp.zeros(out_ref.shape[1:], F32)
    for m in order:
        total = acc3[m, z]
        for k, copy in four[m]:
            copy.wait_recv()
            total = total + r4[k].astype(F32)
        out_ref[m] = total
        square = square + total * total
    sq[0] = jnp.broadcast_to(jnp.sum(square, keepdims=True), sq.shape[1:])
    mine = []
    for off in range(1, Z):
        mine.append(go(sq.at[0], zq.at[off - 1], zsem, off - 1, (lax.rem(z + off, Z), p.lon)))
    whole = sq[0]
    for off, copy in enumerate(mine):
        copy.wait_recv()
        whole = whole + zq[off]
    sq[1] = whole
    mine = []
    for off in range(1, p.L):
        mine.append(go(sq.at[1], lq.at[off - 1], lsem, off - 1, (p.lat, lax.rem(p.lon + off, p.L))))
    for off, copy in enumerate(mine):
        copy.wait_recv()
        whole = whole + lq[off]
    norm = jnp.sqrt(whole[0:1, 0:1]) + 1e-06
    for m in range(many):
        out_ref[m] = out_ref[m] / norm
    for copy in copies:
        copy.wait_send()


def run_step(sizes, latent, cot, weights, where_idx, ids, id_column, source, target, owner):
    Z, Y, X, C = sizes
    L = Y * X * C
    many = len(weights)
    nodes, width = latent.shape
    grid_rows = cot.shape[0]
    blocks, block_len = source.shape
    lanes = -(-3 * nodes // 128) * 128
    R = width // (Z * L)
    w2 = width // 2
    vmem = pl.BlockSpec(memory_space=pltpu.VMEM)

    def buf(dtype, *dims):
        return pltpu.VMEM(dims, dtype)

    def sems(*counts):
        return [pltpu.SemaphoreType.DMA((2, n)) for n in counts]

    nx, ny, nz, nc = many * (X - 1), many * (Y - 1), many * (Z - 1), many * (C - 1)
    second = [buf(BF16, nx, Z, Y, R, w2), buf(BF16, ny, Z, X, R, w2)]
    third = [buf(BF16, ny, Z, R, w2), buf(BF16, nx, Z, R, w2)]
    gathers = (Z - 1) * 2 + Z * (3 * (X - 1) + 3 * (Y - 1) + 2 * (C - 1))
    return pl.pallas_call(
        functools.partial(step_kernel, sizes),
        out_shape=(
            jax.ShapeDtypeStruct((nodes, width), BF16),
            jax.ShapeDtypeStruct((grid_rows, width), BF16),
            jax.ShapeDtypeStruct((many, R, width), F32),
        ),
        in_specs=[vmem] * (8 + many),
        out_specs=(vmem,) * 3,
        scratch_shapes=[
            buf(BF16, Z, Y, X, C, nodes, width), buf(jnp.int32, Z, Y, X, C, *ids.shape),
            buf(BF16, 9 * nodes, width), buf(jnp.int32, 4, 2, CAP, block_len),
            buf(jnp.int32, 2, blocks + 2 * CAP, block_len),
            buf(F32, grid_rows, lanes), buf(BF16, grid_rows, lanes), buf(BF16, grid_rows, lanes),
            buf(BF16, 2, nodes, width), buf(BF16, 2, nodes, width), buf(BF16, lanes, width),
            buf(F32, many, Z, Y, X, C, R, width),
            buf(BF16, nc, Z, Y, X, R, width), buf(BF16, nc, Z, Y, X, R, width),
            buf(F32, many, Z, Y, X, R, width),
            second, second, [buf(F32, many, Z, Y, R, w2), buf(F32, many, Z, X, R, w2)],
            third, third, buf(F32, many, Z, R, width),
            buf(BF16, nz, R, width), buf(BF16, nz, R, width),
            buf(F32, 2, 8, 128), buf(F32, Z - 1, 8, 128), buf(F32, L - 1, 8, 128),
            *sems(gathers, 6, nc), sems(nx, ny), sems(ny, nx), *sems(nz, Z - 1, L - 1),
        ],
        compiler_params=pltpu.CompilerParams(
            collective_id=0, has_side_effects=True, vmem_limit_bytes=60 * 1024 * 1024
        ),
        name="whole_step",
    )(latent, cot, *weights, where_idx, ids, id_column, source, target, owner)


def lon_parts(lat_count, lon_count):
    chips = lon_count // 2
    x = next(d for d in range(math.isqrt(chips), 0, -1) if chips % d == 0)
    return lat_count, chips // x, x, 2


def local(
    mesh_latent,
    grid_cotangent,
    w_source,
    w_target,
    w_node,
    w_coarse,
    w_decode,
    neighbour_codes,
    coarse_ids,
    edge_source,
    edge_target,
    edge_owner,
):
    height, breadth, width = mesh_latent.shape
    nodes = height * breadth
    lat_pos, lon_pos = lax.axis_index("lat"), lax.axis_index("lon")
    lat_count, lon_count = lax.axis_size("lat"), lax.axis_size("lon")
    sizes = lon_parts(lat_count, lon_count)
    rows = jnp.arange(height, dtype=jnp.int32)[None, :, None] + neighbour_codes // 3 - 1
    cols = jnp.arange(breadth, dtype=jnp.int32)[None, None, :] + neighbour_codes % 3 - 1
    below, above = (rows < 0).astype(jnp.int32), (rows >= height).astype(jnp.int32)
    before, after = (cols < 0).astype(jnp.int32), (cols >= breadth).astype(jnp.int32)
    block = (1 + above - below) * 3 + 1 + after - before
    inner = (rows + height * (below - above)) * breadth + cols + breadth * (before - after)
    outside = (below == 1) & (lat_pos == 0) | (above == 1) & (lat_pos == lat_count - 1)
    where_idx = jnp.where(outside, -1, block * nodes + inner).reshape(-1, 1)
    cores = jnp.arange(sizes[3], dtype=jnp.int32)[:, None]
    ids = coarse_ids.reshape(1, nodes) + 1
    id_row = jnp.where(cores == lon_pos % sizes[3], ids, 0).reshape(1, -1)
    blocks = edge_owner.shape[0]
    mesh_out, grid_out, clipped = run_step(
        sizes,
        mesh_latent.reshape(nodes, width),
        grid_cotangent,
        (w_source, w_target, w_node, w_coarse, w_decode),
        where_idx,
        id_row,
        coarse_ids.reshape(nodes, 1) + 1,
        edge_source.reshape(blocks, -1),
        edge_target.reshape(blocks, -1),
        edge_owner,
    )
    return (mesh_out.reshape(height, breadth, width), grid_out, clipped.reshape(clipped.shape[0], -1))


def solution(mesh):
    in_specs = (
        P("lat", "lon", None),
        P(("lat", "lon"), None),
        P(),
        P(),
        P(),
        P(),
        P(),
        P(None, "lat", "lon"),
        P("lat", "lon", None),
        P(("lat", "lon")),
        P(("lat", "lon")),
        P(("lat", "lon"), None),
    )
    out_specs = (P("lat", "lon", None), P(("lat", "lon"), None), P(None, ("lat", "lon")))
    return jax.shard_map(local, mesh=mesh, in_specs=in_specs, out_specs=out_specs, check_vma=False)
```

```python
import functools
import math

import jax
import jax.numpy as jnp
from jax import lax
from jax.experimental import pallas as pl
from jax.experimental.pallas import tpu as pltpu
from jax.sharding import PartitionSpec as P

CAP = 3
F32 = jnp.float32
BF16 = jnp.bfloat16


def silu_slope(value):
    sig = jax.nn.sigmoid(value)
    return sig * (1.0 + value * (1.0 - sig))


def mm(left, right):
    return jnp.dot(left, right, preferred_element_type=F32)


def mm_t(left, right):
    return lax.dot_general(left, right, (((0,), (0,)), ((), ())), preferred_element_type=F32)


def mm_nt(left, right):
    return lax.dot_general(left, right, (((1,), (1,)), ((), ())), preferred_element_type=F32)


def split_float(value):
    high = value.astype(BF16)
    return high, (value - high.astype(F32)).astype(BF16)


MESH = pl.DeviceIdType.MESH


class Place:
    def __init__(self, sizes):
        self.Z, self.Y, self.X, self.C = sizes
        self.L = self.Y * self.X * self.C
        self.lat, self.lon = lax.axis_index("lat"), lax.axis_index("lon")
        self.z, self.c = self.lat, lax.rem(self.lon, self.C)
        self.x = lax.rem(self.lon // self.C, self.X)
        self.y = self.lon // (self.C * self.X)

    def at(self, y=None, x=None, c=None):
        y, x, c = (old if new is None else new for new, old in ((y, self.y), (x, self.x), (c, self.c)))
        return (self.lat, (y * self.X + x) * self.C + c)

    def meet(self):
        barrier = pltpu.get_barrier_semaphore()
        for step in range(1, self.Z):
            peer = (lax.rem(self.z + step, self.Z), self.lon)
            pl.semaphore_signal(barrier, inc=1, device_id=peer, device_id_type=MESH)
        for step in range(1, self.L):
            peer = (self.lat, lax.rem(self.lon + step, self.L))
            pl.semaphore_signal(barrier, inc=1, device_id=peer, device_id_type=MESH)

    def met(self):
        pl.semaphore_wait(pltpu.get_barrier_semaphore(), self.Z - 1 + self.L - 1)


def send(src, dst, sems, slot, peer):
    copy = pltpu.make_async_remote_copy(
        src_ref=src, dst_ref=dst, send_sem=sems.at[0, slot], recv_sem=sems.at[1, slot],
        device_id=peer, device_id_type=MESH,
    )
    copy.start()
    return copy


def iota(shape, dim):
    return lax.broadcasted_iota(jnp.int32, shape, dim)


def step_kernel(sizes, *refs):
    (lat_ref, cot_ref, ws_ref, wt_ref, wn_ref, wc_ref, wd_ref, code_ref, coarse_ref, src_ref, tgt_ref,
     owner_ref) = refs[:12]
    mesh_ref, grid_ref, out_ref = refs[12:15]
    (all_ref, all_id, near, pack, erow, counts, cnt_high, cnt_low, back, backs, msgs, grad, s1, r1, acc1, s2, r2, acc2,
     s3, r3, acc3, s4, r4, sq, zq, lq, id_ref, share) = refs[15:43]
    gsem, esem, sem1, sem2, sem3, sem4, zsem, lsem = refs[43:]
    p = Place(sizes)
    Z, Y, X, C, z, y, x, c = p.Z, p.Y, p.X, p.C, p.z, p.y, p.x, p.c
    nodes, width = lat_ref.shape
    grid_rows = cot_ref.shape[0]
    blocks, block_len = src_ref.shape
    lanes = counts.shape[1]
    to_left = (p.lat, lax.rem(p.lon + p.L - 1, p.L))
    to_right = (p.lat, lax.rem(p.lon + 1, p.L))
    many = out_ref.shape[0]
    R = share.shape[1]
    w2 = width // 2
    halves = (pl.ds(0, w2), pl.ds(w2, w2))
    half = nodes // 2
    low, high = pl.ds(0, half), pl.ds(half, half)
    copies = []
    used = [0]

    def go(src, dst, sems, slot, peer):
        copy = send(src, dst, sems, slot, peer)
        copies.append(copy)
        return copy

    def pass_on(src, dst, peer):
        used[0] += 1
        return go(src, dst, gsem, used[0] - 1, peer)

    p.meet()
    all_ref[z, y, x, c] = lat_ref[...]
    slots, height, breadth = code_ref.shape

    def column(square):
        tall = jnp.concatenate([jnp.broadcast_to(square[i:i + 1], (breadth, breadth)) for i in range(height)], 0)
        keep = iota(tall.shape, 0) % breadth == iota(tall.shape, 1)
        return jnp.sum(jnp.where(keep, tall, 0), 1, keepdims=True)

    id_column = column(coarse_ref[...]) + 1
    spread = (nodes, id_ref.shape[1])
    keep = iota(spread, 1) == iota(spread, 0) + c * nodes
    id_ref[...] = jnp.sum(jnp.where(keep, jnp.broadcast_to(id_column, spread), 0), 0, keepdims=True)
    all_id[z, y, x, c] = id_ref[...]
    sub, lane = iota((blocks, blocks), 0), iota((blocks, blocks), 1)
    owner = jnp.broadcast_to(owner_ref[...], (blocks, blocks))
    owner = jnp.sum(jnp.where(sub == lane, owner, 0), 1, keepdims=True)
    is_left = (owner == lax.rem(p.lon + p.L - 1, p.L)).astype(jnp.int32)
    is_right = (owner == lax.rem(p.lon + 1, p.L)).astype(jnp.int32)

    def ranks(column):
        row = jnp.sum(jnp.where(sub == lane, jnp.broadcast_to(column, sub.shape), 0), 0, keepdims=True)
        return jnp.sum(jnp.where(lane < sub, jnp.broadcast_to(row, sub.shape), 0), 1, keepdims=True)

    place = jnp.where(is_left == 1, ranks(is_left), jnp.where(is_right == 1, CAP + ranks(is_right), -1))
    wide_place = jnp.broadcast_to(place, (blocks, block_len))
    for r in range(2 * CAP):
        mine = wide_place == r
        side, row = divmod(r, CAP)
        pack[side, 0, row:row + 1] = jnp.sum(jnp.where(mine, src_ref[...], 0), 0, keepdims=True)
        pack[side, 1, row:row + 1] = jnp.sum(jnp.where(mine, tgt_ref[...] + 1, 0), 0, keepdims=True) - 1
    p.met()
    first = []
    for step in range(1, Z):
        peer = (lax.rem(z + step, Z), p.lon)
        first.append([
            pass_on(lat_ref, all_ref.at[z, y, x, c], peer),
            pass_on(id_ref, all_id.at[z, y, x, c], peer),
        ])
    edges = [go(pack.at[0], pack.at[3], esem, 0, to_left), go(pack.at[1], pack.at[2], esem, 1, to_right)]
    second, third, fourth = [], [], []

    def hop_two(step):
        line = lax.rem(z + Z - step, Z)
        if step:
            for copy in first[step - 1]:
                copy.wait_recv()
        mine = []
        block = all_ref.at[line, y, x, c]
        src_low = block.at[low] if step else lat_ref.at[low]
        src_high = block.at[high] if step else lat_ref.at[high]
        src_id = all_id.at[line, y, x, c] if step else id_ref
        for off in range(1, X):
            peer = p.at(x=lax.rem(x + off, X))
            mine.append(pass_on(src_low, block.at[low], peer))
            mine.append(pass_on(src_id, all_id.at[line, y, x, c], peer))
        for off in range(1, Y):
            mine.append(pass_on(src_high, block.at[high], p.at(y=lax.rem(y + off, Y))))
        second.append(mine)

    def hop_three(step):
        line = lax.rem(z + Z - step, Z)
        for copy in second[step]:
            copy.wait_recv()
        mine = []
        for off in range(1, Y):
            peer = p.at(y=lax.rem(y + off, Y))
            part = all_ref.at[line, y, :, c, low]
            mine.append(pass_on(part, part, peer))
            part = all_id.at[line, y, :, c]
            mine.append(pass_on(part, part, peer))
        for off in range(1, X):
            part = all_ref.at[line, :, x, c, high]
            mine.append(pass_on(part, part, p.at(x=lax.rem(x + off, X))))
        third.append(mine)

    def hop_four(step):
        line = lax.rem(z + Z - step, Z)
        for copy in third[step]:
            copy.wait_recv()
        mine = []
        for off in range(1, C):
            peer = p.at(c=lax.rem(c + off, C))
            part = all_ref.at[line, :, :, c]
            mine.append(pass_on(part, part, peer))
            part = all_id.at[line, :, :, c]
            mine.append(pass_on(part, part, peer))
        fourth.append(mine)

    stays = jnp.broadcast_to((owner == p.lon).astype(jnp.int32), (blocks, block_len))
    erow[0, 0:blocks] = src_ref[...]
    erow[1, 0:blocks] = jnp.where(stays == 1, tgt_ref[...], -1)
    pair = 2 if blocks % 2 == 0 else 1

    def count(start, stop):
        for b in range(start, stop, pair):
            upto = min(b + pair, stop)
            tgt = jnp.concatenate([jnp.broadcast_to(erow[1, r:r + 1], (grid_rows, block_len)) for r in range(b, upto)], 1)
            src = jnp.concatenate([jnp.broadcast_to(erow[0, r:r + 1], (lanes, block_len)) for r in range(b, upto)], 1)
            hot_t = jnp.where(tgt == iota(tgt.shape, 0), 1.0, 0.0).astype(BF16)
            hot_s = jnp.where(src == iota(src.shape, 0), 1.0, 0.0).astype(BF16)
            more = mm_nt(hot_t, hot_s)
            counts[...] = more if b == 0 else counts[...] + more

    quarter = blocks // 4 // pair * pair
    hop_two(0)
    count(0, quarter)
    for step in range(1, Z):
        hop_two(step)
    count(quarter, 2 * quarter)
    for step in range(Z):
        hop_three(step)
    count(2 * quarter, 3 * quarter)
    for step in range(Z):
        hop_four(step)
    count(3 * quarter, blocks)
    for copy in edges:
        copy.wait_recv()
    for side in range(2):
        erow[0, blocks + side * CAP:blocks + (side + 1) * CAP] = pack[2 + side, 0] + (side + 1) * nodes
        erow[1, blocks + side * CAP:blocks + (side + 1) * CAP] = pack[2 + side, 1]
    count(blocks, blocks + 2 * CAP)
    over = jnp.floor(counts[...] * (1.0 / 256.0)) * 256.0
    cnt_high[...] = over.astype(BF16)
    cnt_low[...] = (counts[...] - over).astype(BF16)
    cot_sums = mm_t(cnt_high[...], cot_ref[...]) + mm_t(cnt_low[...], cot_ref[...])
    backs[0] = cot_sums[nodes:2 * nodes].astype(BF16)
    backs[1] = cot_sums[2 * nodes:3 * nodes].astype(BF16)
    returns = [go(backs.at[0], back.at[0], esem, 2, to_left), go(backs.at[1], back.at[1], esem, 3, to_right)]
    latent = lat_ref[...]
    toward = mm(latent, wt_ref[...])

    pooled = jnp.zeros((nodes, width), F32)
    count_of = jnp.zeros((nodes, 1), F32)
    for step in range(Z):
        line = lax.rem(z + Z - step, Z)
        for copy in fourth[step]:
            copy.wait_recv()
        ids = jnp.sum(all_id[line].reshape(Y * X, C, C * nodes), 1)
        row = jnp.concatenate([ids[q:q + 1] for q in range(Y * X)], 1)
        wide = jnp.broadcast_to(row, (nodes, row.shape[1]))
        same = jnp.where(wide == jnp.broadcast_to(id_column, wide.shape), 1.0, 0.0)
        count_of = count_of + jnp.sum(same, 1, keepdims=True)
        pooled = pooled + mm(same.astype(BF16), all_ref[line].reshape(p.L * nodes, width))
    coarse_in = (pooled * lax.rsqrt(count_of)).astype(BF16)
    cpre = mm(coarse_in, wc_ref[...])
    coarse_out = (cpre * jax.nn.sigmoid(cpre)).astype(BF16)

    for r in range(3):
        for q in range(3):
            lon = lax.rem(p.lon + q - 1 + p.L, p.L)
            line = lax.rem(z + r - 1 + Z, Z)
            block = all_ref[line, lon // (C * X), lax.rem(lon // C, X), lax.rem(lon, C)]
            near[(r * 3 + q) * nodes:(r * 3 + q + 1) * nodes] = block
    at_row, at_col = iota((height, breadth), 0), iota((height, breadth), 1)
    wheres = []
    for k in range(slots):
        code = code_ref[k]
        down = jnp.where(code >= 6, 1, jnp.where(code >= 3, 0, -1))
        rows, cols = at_row + down, at_col + code - 3 * down - 4
        below, above = jnp.where(rows < 0, 1, 0), jnp.where(rows >= height, 1, 0)
        before, after = jnp.where(cols < 0, 1, 0), jnp.where(cols >= breadth, 1, 0)
        block = (1 + above - below) * 3 + 1 + after - before
        inner = (rows + height * (below - above)) * breadth + cols + breadth * (before - after)
        first_line, last_line = jnp.where(z == 0, 1, 0), jnp.where(z == Z - 1, 1, 0)
        outside = below * first_line + above * last_line
        wheres.append(column(jnp.where(outside > 0, -1, block * nodes + inner)))
    where = jnp.concatenate(wheres, 0)
    hot = jnp.broadcast_to(where, (where.shape[0], near.shape[0]))
    hot = jnp.where(hot == iota(hot.shape, 1), 1.0, 0.0).astype(BF16)
    beside = mm(hot, near[...]).astype(BF16)
    edges_pre = mm(beside, ws_ref[...]).reshape(slots, nodes, width) + toward[None]
    agg = jnp.sum(edges_pre * jax.nn.sigmoid(edges_pre), 0).astype(BF16)

    npre = mm(agg, wn_ref[...]) + coarse_out.astype(F32)
    mesh_out = (latent.astype(F32) + npre * jax.nn.sigmoid(npre)).astype(BF16)
    mesh_ref[...] = mesh_out

    pre = mm(mesh_out, wd_ref[...])
    msgs[0:nodes] = (pre * jax.nn.sigmoid(pre)).astype(BF16)
    if lanes > 3 * nodes:
        msgs[3 * nodes:] = jnp.zeros((lanes - 3 * nodes, width), BF16)
    mine = msgs.at[pl.ds(0, nodes)]
    spoken = [
        go(mine, msgs.at[pl.ds(nodes, nodes)], esem, 4, to_right),
        go(mine, msgs.at[pl.ds(2 * nodes, nodes)], esem, 5, to_left),
    ]

    one, two, three, four = {}, {}, {}, {}

    def hop_core(m, value):
        if R % 8 == 0:
            grad[m] = value.reshape(Z, Y, X, C, R, width)
        else:
            for q in range(Z * p.L):
                spot = (q // p.L, q // (C * X) % Y, q // C % X, q % C)
                grad[(m, *spot)] = value[q * R:(q + 1) * R]
        one[m] = []
        for off in range(1, C):
            there = lax.rem(c + off, C)
            k = m * (C - 1) + off - 1
            s1[k] = grad[m, :, :, :, there].astype(BF16)
            one[m].append((k, go(s1.at[k], r1.at[k], sem1, k, p.at(c=there))))

    def hop_first(m):
        total = grad[m, :, :, :, c]
        for k, copy in one[m]:
            copy.wait_recv()
            total = total + r1[k].astype(F32)
        acc1[m] = total
        two[m] = ([], [])
        for off in range(1, X):
            there = lax.rem(x + off, X)
            k = m * (X - 1) + off - 1
            s2[0][k] = acc1[m, :, :, there, :, halves[0]].astype(BF16)
            two[m][0].append((k, go(s2[0].at[k], r2[0].at[k], sem2[0], k, p.at(x=there))))
        for off in range(1, Y):
            there = lax.rem(y + off, Y)
            k = m * (Y - 1) + off - 1
            s2[1][k] = acc1[m, :, there, :, :, halves[1]].astype(BF16)
            two[m][1].append((k, go(s2[1].at[k], r2[1].at[k], sem2[1], k, p.at(y=there))))

    def hop_other(m):
        three[m] = ([], [])
        total = acc1[m, :, :, x, :, halves[0]]
        for k, copy in two[m][0]:
            copy.wait_recv()
            total = total + r2[0][k].astype(F32)
        acc2[0][m] = total
        for off in range(1, Y):
            there = lax.rem(y + off, Y)
            k = m * (Y - 1) + off - 1
            s3[0][k] = acc2[0][m, :, there].astype(BF16)
            three[m][0].append((k, go(s3[0].at[k], r3[0].at[k], sem3[0], k, p.at(y=there))))
        total = acc1[m, :, y, :, :, halves[1]]
        for k, copy in two[m][1]:
            copy.wait_recv()
            total = total + r2[1][k].astype(F32)
        acc2[1][m] = total
        for off in range(1, X):
            there = lax.rem(x + off, X)
            k = m * (X - 1) + off - 1
            s3[1][k] = acc2[1][m, :, there].astype(BF16)
            three[m][1].append((k, go(s3[1].at[k], r3[1].at[k], sem3[1], k, p.at(x=there))))

    def hop_line(m):
        for side, own in ((0, y), (1, x)):
            total = acc2[side][m, :, own]
            for k, copy in three[m][side]:
                copy.wait_recv()
                total = total + r3[side][k].astype(F32)
            acc3[m, :, :, halves[side]] = total
        four[m] = []
        for off in range(1, Z):
            there = lax.rem(z + off, Z)
            k = m * (Z - 1) + off - 1
            s4[k] = acc3[m, there].astype(BF16)
            four[m].append((k, go(s4.at[k], r4.at[k], sem4, k, (there, p.lon))))

    for copy in returns:
        copy.wait_recv()
    cot_sum = cot_sums[:nodes] + back[0].astype(F32) + back[1].astype(F32)
    d_high, d_low = split_float(cot_sum * silu_slope(pre))
    hop_core(4, mm_t(mesh_out, d_high) + mm_t(mesh_out, d_low))
    d_node = (mm_nt(d_high, wd_ref[...]) * silu_slope(npre)).astype(BF16)
    hop_core(2, mm_t(agg, d_node))
    hop_first(4)
    c_high, c_low = split_float(d_node.astype(F32) * silu_slope(cpre))
    hop_core(3, mm_t(coarse_in, c_high) + mm_t(coarse_in, c_low))
    hop_first(2)
    d_edges = (mm_nt(d_node, wn_ref[...])[None] * silu_slope(edges_pre)).astype(BF16)
    d_sum = jnp.sum(d_edges.astype(F32), 0).astype(BF16)
    hop_core(1, mm_t(latent, d_sum))
    hop_first(3)
    hop_core(0, mm_t(beside, d_edges.reshape(slots * nodes, width)))
    hop_first(1)
    hop_first(0)
    order = (4, 2, 3, 1, 0)
    hop_other(order[0])
    for copy in spoken:
        copy.wait_recv()
    grid_ref[...] = (mm(cnt_high[...], msgs[...]) + mm(cnt_low[...], msgs[...])).astype(BF16)
    for m in order[1:]:
        hop_other(m)
    for m in order:
        hop_line(m)
    square = jnp.zeros(share.shape[1:], F32)
    for m in order:
        total = acc3[m, z]
        for k, copy in four[m]:
            copy.wait_recv()
            total = total + r4[k].astype(F32)
        share[m] = total
        square = square + total * total
    sq[0] = jnp.broadcast_to(jnp.sum(square, keepdims=True), sq.shape[1:])
    mine = []
    for off in range(1, Z):
        mine.append(go(sq.at[0], zq.at[off - 1], zsem, off - 1, (lax.rem(z + off, Z), p.lon)))
    whole = sq[0]
    for off, copy in enumerate(mine):
        copy.wait_recv()
        whole = whole + zq[off]
    sq[1] = whole
    mine = []
    for off in range(1, p.L):
        mine.append(go(sq.at[1], lq.at[off - 1], lsem, off - 1, (p.lat, lax.rem(p.lon + off, p.L))))
    for off, copy in enumerate(mine):
        copy.wait_recv()
        whole = whole + lq[off]
    norm = jnp.sqrt(whole[0:1, 0:1]) + 1e-06
    for m in range(many):
        total = share[m] / norm
        for r in range(R):
            out_ref[m:m + 1, r * width:(r + 1) * width] = total[r:r + 1]
    for copy in copies:
        copy.wait_send()


def run_step(sizes, latent, cot, weights, codes, ids, source, target, owner):
    Z, Y, X, C = sizes
    L = Y * X * C
    many = len(weights)
    nodes, width = latent.shape
    grid_rows = cot.shape[0]
    blocks, block_len = source.shape
    lanes = -(-3 * nodes // 128) * 128
    R = width // (Z * L)
    w2 = width // 2
    vmem = pl.BlockSpec(memory_space=pltpu.VMEM)

    def buf(dtype, *dims):
        return pltpu.VMEM(dims, dtype)

    def sems(*counts):
        return [pltpu.SemaphoreType.DMA((2, n)) for n in counts]

    nx, ny, nz, nc = many * (X - 1), many * (Y - 1), many * (Z - 1), many * (C - 1)
    second = [buf(BF16, nx, Z, Y, R, w2), buf(BF16, ny, Z, X, R, w2)]
    third = [buf(BF16, ny, Z, R, w2), buf(BF16, nx, Z, R, w2)]
    gathers = (Z - 1) * 2 + Z * (3 * (X - 1) + 3 * (Y - 1) + 2 * (C - 1))
    return pl.pallas_call(
        functools.partial(step_kernel, sizes),
        out_shape=(
            jax.ShapeDtypeStruct((nodes, width), BF16),
            jax.ShapeDtypeStruct((grid_rows, width), BF16),
            jax.ShapeDtypeStruct((many, R * width), F32),
        ),
        in_specs=[vmem] * (7 + many),
        out_specs=(vmem,) * 3,
        scratch_shapes=[
            buf(BF16, Z, Y, X, C, nodes, width), buf(jnp.int32, Z, Y, X, C, 1, C * nodes),
            buf(BF16, 9 * nodes, width), buf(jnp.int32, 4, 2, CAP, block_len),
            buf(jnp.int32, 2, blocks + 2 * CAP, block_len),
            buf(F32, grid_rows, lanes), buf(BF16, grid_rows, lanes), buf(BF16, grid_rows, lanes),
            buf(BF16, 2, nodes, width), buf(BF16, 2, nodes, width), buf(BF16, lanes, width),
            buf(F32, many, Z, Y, X, C, R, width),
            buf(BF16, nc, Z, Y, X, R, width), buf(BF16, nc, Z, Y, X, R, width),
            buf(F32, many, Z, Y, X, R, width),
            second, second, [buf(F32, many, Z, Y, R, w2), buf(F32, many, Z, X, R, w2)],
            third, third, buf(F32, many, Z, R, width),
            buf(BF16, nz, R, width), buf(BF16, nz, R, width),
            buf(F32, 2, 8, 128), buf(F32, Z - 1, 8, 128), buf(F32, L - 1, 8, 128),
            buf(jnp.int32, 1, C * nodes), buf(F32, many, R, width),
            *sems(gathers, 6, nc), sems(nx, ny), sems(ny, nx), *sems(nz, Z - 1, L - 1),
        ],
        compiler_params=pltpu.CompilerParams(
            collective_id=0, has_side_effects=True, vmem_limit_bytes=60 * 1024 * 1024
        ),
        name="whole_step",
    )(latent, cot, *weights, codes, ids, source, target, owner)


def lon_parts(lat_count, lon_count):
    chips = lon_count // 2
    x = next(d for d in range(math.isqrt(chips), 0, -1) if chips % d == 0)
    return lat_count, chips // x, x, 2


def local(
    mesh_latent,
    grid_cotangent,
    w_source,
    w_target,
    w_node,
    w_coarse,
    w_decode,
    neighbour_codes,
    coarse_ids,
    edge_source,
    edge_target,
    edge_owner,
):
    height, breadth, width = mesh_latent.shape
    nodes = height * breadth
    sizes = lon_parts(lax.axis_size("lat"), lax.axis_size("lon"))
    blocks = edge_owner.shape[0]
    mesh_out, grid_out, clipped = run_step(
        sizes,
        mesh_latent.reshape(nodes, width),
        grid_cotangent,
        (w_source, w_target, w_node, w_coarse, w_decode),
        neighbour_codes,
        coarse_ids.reshape(height, breadth),
        edge_source.reshape(blocks, -1),
        edge_target.reshape(blocks, -1),
        edge_owner.reshape(1, blocks),
    )
    return (mesh_out.reshape(height, breadth, width), grid_out, clipped)


def solution(mesh):
    in_specs = (
        P("lat", "lon", None),
        P(("lat", "lon"), None),
        P(),
        P(),
        P(),
        P(),
        P(),
        P(None, "lat", "lon"),
        P("lat", "lon", None),
        P(("lat", "lon")),
        P(("lat", "lon")),
        P(("lat", "lon"), None),
    )
    out_specs = (P("lat", "lon", None), P(("lat", "lon"), None), P(None, ("lat", "lon")))
    return jax.shard_map(local, mesh=mesh, in_specs=in_specs, out_specs=out_specs, check_vma=False)
```

```python
import functools
import math

import jax
import jax.numpy as jnp
from jax import lax
from jax.experimental import pallas as pl
from jax.experimental.pallas import tpu as pltpu
from jax.sharding import PartitionSpec as P

CAP = 3
F32 = jnp.float32
BF16 = jnp.bfloat16


def silu_slope(value):
    sig = jax.nn.sigmoid(value)
    return sig * (1.0 + value * (1.0 - sig))


def mm(left, right):
    return jnp.dot(left, right, preferred_element_type=F32)


def mm_t(left, right):
    return lax.dot_general(left, right, (((0,), (0,)), ((), ())), preferred_element_type=F32)


def mm_nt(left, right):
    return lax.dot_general(left, right, (((1,), (1,)), ((), ())), preferred_element_type=F32)


def split_float(value):
    high = value.astype(BF16)
    return high, (value - high.astype(F32)).astype(BF16)


MESH = pl.DeviceIdType.MESH


class Place:
    def __init__(self, sizes):
        self.Z, self.Y, self.X, self.C = sizes
        self.L = self.Y * self.X * self.C
        self.lat, self.lon = lax.axis_index("lat"), lax.axis_index("lon")
        self.z, self.c = self.lat, lax.rem(self.lon, self.C)
        self.x = lax.rem(self.lon // self.C, self.X)
        self.y = self.lon // (self.C * self.X)

    def at(self, y=None, x=None, c=None):
        y, x, c = (old if new is None else new for new, old in ((y, self.y), (x, self.x), (c, self.c)))
        return (self.lat, (y * self.X + x) * self.C + c)

    def meet(self):
        barrier = pltpu.get_barrier_semaphore()
        for step in range(1, self.Z):
            peer = (lax.rem(self.z + step, self.Z), self.lon)
            pl.semaphore_signal(barrier, inc=1, device_id=peer, device_id_type=MESH)
        for step in range(1, self.L):
            peer = (self.lat, lax.rem(self.lon + step, self.L))
            pl.semaphore_signal(barrier, inc=1, device_id=peer, device_id_type=MESH)

    def met(self):
        pl.semaphore_wait(pltpu.get_barrier_semaphore(), self.Z - 1 + self.L - 1)


def send(src, dst, sems, slot, peer):
    copy = pltpu.make_async_remote_copy(
        src_ref=src, dst_ref=dst, send_sem=sems.at[0, slot], recv_sem=sems.at[1, slot],
        device_id=peer, device_id_type=MESH,
    )
    copy.start()
    return copy


def iota(shape, dim):
    return lax.broadcasted_iota(jnp.int32, shape, dim)


def step_kernel(sizes, *refs):
    (lat_ref, cot_ref, ws_ref, wt_ref, wn_ref, wc_ref, wd_ref, code_ref, coarse_ref, src_ref, tgt_ref,
     owner_ref) = refs[:12]
    mesh_ref, grid_ref, out_ref = refs[12:15]
    (all_ref, all_id, near, pack, erow, counts, cnt_high, cnt_low, back, backs, msgs, grad, s1, r1, acc1, s2, r2, acc2,
     s3, r3, acc3, s4, r4, sq, zq, lq, id_ref, share) = refs[15:43]
    gsem, esem, sem1, sem2, sem3, sem4, zsem, lsem = refs[43:]
    p = Place(sizes)
    Z, Y, X, C, z, y, x, c = p.Z, p.Y, p.X, p.C, p.z, p.y, p.x, p.c
    nodes, width = lat_ref.shape
    grid_rows = cot_ref.shape[0]
    blocks, block_len = src_ref.shape
    lanes = counts.shape[1]
    to_left = (p.lat, lax.rem(p.lon + p.L - 1, p.L))
    to_right = (p.lat, lax.rem(p.lon + 1, p.L))
    many = out_ref.shape[0]
    R = share.shape[1]
    w2 = width // 2
    halves = (pl.ds(0, w2), pl.ds(w2, w2))
    half = nodes // 2
    low, high = pl.ds(0, half), pl.ds(half, half)
    copies = []
    used = [0]

    def go(src, dst, sems, slot, peer):
        copy = send(src, dst, sems, slot, peer)
        copies.append(copy)
        return copy

    def pass_on(src, dst, peer):
        used[0] += 1
        return go(src, dst, gsem, used[0] - 1, peer)

    p.meet()
    all_ref[z, y, x, c] = lat_ref[...]
    slots, height, breadth = code_ref.shape

    def column(square):
        tall = jnp.concatenate([jnp.broadcast_to(square[i:i + 1], (breadth, breadth)) for i in range(height)], 0)
        keep = iota(tall.shape, 0) % breadth == iota(tall.shape, 1)
        return jnp.sum(jnp.where(keep, tall, 0), 1, keepdims=True)

    id_column = column(coarse_ref[...]) + 1
    spread = (nodes, id_ref.shape[1])
    keep = iota(spread, 1) == iota(spread, 0) + c * nodes
    id_ref[...] = jnp.sum(jnp.where(keep, jnp.broadcast_to(id_column, spread), 0), 0, keepdims=True)
    all_id[z, y, x, c] = id_ref[...]
    sub, lane = iota((blocks, blocks), 0), iota((blocks, blocks), 1)
    owner = jnp.broadcast_to(owner_ref[...], (blocks, blocks))
    owner = jnp.sum(jnp.where(sub == lane, owner, 0), 1, keepdims=True)
    is_left = (owner == lax.rem(p.lon + p.L - 1, p.L)).astype(jnp.int32)
    is_right = (owner == lax.rem(p.lon + 1, p.L)).astype(jnp.int32)

    def ranks(column):
        row = jnp.sum(jnp.where(sub == lane, jnp.broadcast_to(column, sub.shape), 0), 0, keepdims=True)
        return jnp.sum(jnp.where(lane < sub, jnp.broadcast_to(row, sub.shape), 0), 1, keepdims=True)

    place = jnp.where(is_left == 1, ranks(is_left), jnp.where(is_right == 1, CAP + ranks(is_right), -1))
    wide_place = jnp.broadcast_to(place, (blocks, block_len))
    for r in range(2 * CAP):
        mine = wide_place == r
        side, row = divmod(r, CAP)
        pack[side, 0, row:row + 1] = jnp.sum(jnp.where(mine, src_ref[...], 0), 0, keepdims=True)
        pack[side, 1, row:row + 1] = jnp.sum(jnp.where(mine, tgt_ref[...] + 1, 0), 0, keepdims=True) - 1
    p.met()
    first = []
    for step in range(1, Z):
        peer = (lax.rem(z + step, Z), p.lon)
        first.append([
            pass_on(lat_ref, all_ref.at[z, y, x, c], peer),
            pass_on(id_ref, all_id.at[z, y, x, c], peer),
        ])
    edges = [go(pack.at[0], pack.at[3], esem, 0, to_left), go(pack.at[1], pack.at[2], esem, 1, to_right)]
    second, third, fourth = [], [], []

    def hop_two(step):
        line = lax.rem(z + Z - step, Z)
        if step:
            for copy in first[step - 1]:
                copy.wait_recv()
        mine = []
        block = all_ref.at[line, y, x, c]
        src_low = block.at[low] if step else lat_ref.at[low]
        src_high = block.at[high] if step else lat_ref.at[high]
        src_id = all_id.at[line, y, x, c] if step else id_ref
        for off in range(1, X):
            peer = p.at(x=lax.rem(x + off, X))
            mine.append(pass_on(src_low, block.at[low], peer))
            mine.append(pass_on(src_id, all_id.at[line, y, x, c], peer))
        for off in range(1, Y):
            mine.append(pass_on(src_high, block.at[high], p.at(y=lax.rem(y + off, Y))))
        second.append(mine)

    def hop_three(step):
        line = lax.rem(z + Z - step, Z)
        for copy in second[step]:
            copy.wait_recv()
        mine = []
        for off in range(1, Y):
            peer = p.at(y=lax.rem(y + off, Y))
            part = all_ref.at[line, y, :, c, low]
            mine.append(pass_on(part, part, peer))
            part = all_id.at[line, y, :, c]
            mine.append(pass_on(part, part, peer))
        for off in range(1, X):
            part = all_ref.at[line, :, x, c, high]
            mine.append(pass_on(part, part, p.at(x=lax.rem(x + off, X))))
        third.append(mine)

    def hop_four(step):
        line = lax.rem(z + Z - step, Z)
        for copy in third[step]:
            copy.wait_recv()
        mine = []
        for off in range(1, C):
            peer = p.at(c=lax.rem(c + off, C))
            part = all_ref.at[line, :, :, c]
            mine.append(pass_on(part, part, peer))
            part = all_id.at[line, :, :, c]
            mine.append(pass_on(part, part, peer))
        fourth.append(mine)

    stays = jnp.broadcast_to((owner == p.lon).astype(jnp.int32), (blocks, block_len))
    erow[0, 0:blocks] = src_ref[...]
    erow[1, 0:blocks] = jnp.where(stays == 1, tgt_ref[...], -1)
    pair = 2 if blocks % 2 == 0 else 1

    def count(start, stop):
        for b in range(start, stop, pair):
            upto = min(b + pair, stop)
            tgt = jnp.concatenate([jnp.broadcast_to(erow[1, r:r + 1], (grid_rows, block_len)) for r in range(b, upto)], 1)
            src = jnp.concatenate([jnp.broadcast_to(erow[0, r:r + 1], (lanes, block_len)) for r in range(b, upto)], 1)
            hot_t = jnp.where(tgt == iota(tgt.shape, 0), 1.0, 0.0).astype(BF16)
            hot_s = jnp.where(src == iota(src.shape, 0), 1.0, 0.0).astype(BF16)
            more = mm_nt(hot_t, hot_s)
            counts[...] = more if b == 0 else counts[...] + more

    quarter = blocks // 4 // pair * pair
    hop_two(0)
    count(0, quarter)
    for step in range(1, Z):
        hop_two(step)
    count(quarter, 2 * quarter)
    for step in range(Z):
        hop_three(step)
    count(2 * quarter, 3 * quarter)
    for step in range(Z):
        hop_four(step)
    count(3 * quarter, blocks)
    for copy in edges:
        copy.wait_recv()
    for side in range(2):
        erow[0, blocks + side * CAP:blocks + (side + 1) * CAP] = pack[2 + side, 0] + (side + 1) * nodes
        erow[1, blocks + side * CAP:blocks + (side + 1) * CAP] = pack[2 + side, 1]
    count(blocks, blocks + 2 * CAP)
    over = jnp.floor(counts[...] * (1.0 / 256.0)) * 256.0
    cnt_high[...] = over.astype(BF16)
    cnt_low[...] = (counts[...] - over).astype(BF16)
    cot_sums = mm_t(cnt_high[...], cot_ref[...]) + mm_t(cnt_low[...], cot_ref[...])
    backs[0] = cot_sums[nodes:2 * nodes].astype(BF16)
    backs[1] = cot_sums[2 * nodes:3 * nodes].astype(BF16)
    returns = [go(backs.at[0], back.at[0], esem, 2, to_left), go(backs.at[1], back.at[1], esem, 3, to_right)]
    latent = lat_ref[...]
    toward = mm(latent, wt_ref[...])

    pooled = jnp.zeros((nodes, width), F32)
    count_of = jnp.zeros((nodes, 1), F32)
    for step in range(Z):
        line = lax.rem(z + Z - step, Z)
        for copy in fourth[step]:
            copy.wait_recv()
        ids = jnp.sum(all_id[line].reshape(Y * X, C, C * nodes), 1)
        row = jnp.concatenate([ids[q:q + 1] for q in range(Y * X)], 1)
        wide = jnp.broadcast_to(row, (nodes, row.shape[1]))
        same = jnp.where(wide == jnp.broadcast_to(id_column, wide.shape), 1.0, 0.0)
        count_of = count_of + jnp.sum(same, 1, keepdims=True)
        pooled = pooled + mm(same.astype(BF16), all_ref[line].reshape(p.L * nodes, width))
    coarse_in = (pooled * lax.rsqrt(count_of)).astype(BF16)
    cpre = mm(coarse_in, wc_ref[...])
    coarse_out = (cpre * jax.nn.sigmoid(cpre)).astype(BF16)

    for r in range(3):
        for q in range(3):
            lon = lax.rem(p.lon + q - 1 + p.L, p.L)
            line = lax.rem(z + r - 1 + Z, Z)
            block = all_ref[line, lon // (C * X), lax.rem(lon // C, X), lax.rem(lon, C)]
            near[(r * 3 + q) * nodes:(r * 3 + q + 1) * nodes] = block
    at_row, at_col = iota((height, breadth), 0), iota((height, breadth), 1)
    wheres = []
    for k in range(slots):
        code = code_ref[k]
        down = jnp.where(code >= 6, 1, jnp.where(code >= 3, 0, -1))
        rows, cols = at_row + down, at_col + code - 3 * down - 4
        below, above = jnp.where(rows < 0, 1, 0), jnp.where(rows >= height, 1, 0)
        before, after = jnp.where(cols < 0, 1, 0), jnp.where(cols >= breadth, 1, 0)
        block = (1 + above - below) * 3 + 1 + after - before
        inner = (rows + height * (below - above)) * breadth + cols + breadth * (before - after)
        first_line, last_line = jnp.where(z == 0, 1, 0), jnp.where(z == Z - 1, 1, 0)
        outside = below * first_line + above * last_line
        wheres.append(column(jnp.where(outside > 0, -1, block * nodes + inner)))
    where = jnp.concatenate(wheres, 0)
    hot = jnp.broadcast_to(where, (where.shape[0], near.shape[0]))
    hot = jnp.where(hot == iota(hot.shape, 1), 1.0, 0.0).astype(BF16)
    beside = mm(hot, near[...]).astype(BF16)
    edges_pre = mm(beside, ws_ref[...]).reshape(slots, nodes, width) + toward[None]
    agg = jnp.sum(edges_pre * jax.nn.sigmoid(edges_pre), 0).astype(BF16)

    npre = mm(agg, wn_ref[...]) + coarse_out.astype(F32)
    mesh_out = (latent.astype(F32) + npre * jax.nn.sigmoid(npre)).astype(BF16)
    mesh_ref[...] = mesh_out

    pre = mm(mesh_out, wd_ref[...])
    msgs[0:nodes] = (pre * jax.nn.sigmoid(pre)).astype(BF16)
    if lanes > 3 * nodes:
        msgs[3 * nodes:] = jnp.zeros((lanes - 3 * nodes, width), BF16)
    mine = msgs.at[pl.ds(0, nodes)]
    spoken = [
        go(mine, msgs.at[pl.ds(nodes, nodes)], esem, 4, to_right),
        go(mine, msgs.at[pl.ds(2 * nodes, nodes)], esem, 5, to_left),
    ]

    one, two, three, four = {}, {}, {}, {}

    def hop_core(m, value):
        if R % 8 == 0:
            grad[m] = value.reshape(Z, Y, X, C, R, width)
        else:
            for q in range(Z * p.L):
                spot = (q // p.L, q // (C * X) % Y, q // C % X, q % C)
                grad[(m, *spot)] = value[q * R:(q + 1) * R]
        one[m] = []
        for off in range(1, C):
            there = lax.rem(c + off, C)
            k = m * (C - 1) + off - 1
            s1[k] = grad[m, :, :, :, there].astype(BF16)
            one[m].append((k, go(s1.at[k], r1.at[k], sem1, k, p.at(c=there))))

    def hop_first(m):
        total = grad[m, :, :, :, c]
        for k, copy in one[m]:
            copy.wait_recv()
            total = total + r1[k].astype(F32)
        acc1[m] = total
        two[m] = ([], [])
        for off in range(1, X):
            there = lax.rem(x + off, X)
            k = m * (X - 1) + off - 1
            s2[0][k] = acc1[m, :, :, there, :, halves[0]].astype(BF16)
            two[m][0].append((k, go(s2[0].at[k], r2[0].at[k], sem2[0], k, p.at(x=there))))
        for off in range(1, Y):
            there = lax.rem(y + off, Y)
            k = m * (Y - 1) + off - 1
            s2[1][k] = acc1[m, :, there, :, :, halves[1]].astype(BF16)
            two[m][1].append((k, go(s2[1].at[k], r2[1].at[k], sem2[1], k, p.at(y=there))))

    def hop_other(m):
        three[m] = ([], [])
        total = acc1[m, :, :, x, :, halves[0]]
        for k, copy in two[m][0]:
            copy.wait_recv()
            total = total + r2[0][k].astype(F32)
        acc2[0][m] = total
        for off in range(1, Y):
            there = lax.rem(y + off, Y)
            k = m * (Y - 1) + off - 1
            s3[0][k] = acc2[0][m, :, there].astype(BF16)
            three[m][0].append((k, go(s3[0].at[k], r3[0].at[k], sem3[0], k, p.at(y=there))))
        total = acc1[m, :, y, :, :, halves[1]]
        for k, copy in two[m][1]:
            copy.wait_recv()
            total = total + r2[1][k].astype(F32)
        acc2[1][m] = total
        for off in range(1, X):
            there = lax.rem(x + off, X)
            k = m * (X - 1) + off - 1
            s3[1][k] = acc2[1][m, :, there].astype(BF16)
            three[m][1].append((k, go(s3[1].at[k], r3[1].at[k], sem3[1], k, p.at(x=there))))

    def hop_line(m):
        for side, own in ((0, y), (1, x)):
            total = acc2[side][m, :, own]
            for k, copy in three[m][side]:
                copy.wait_recv()
                total = total + r3[side][k].astype(F32)
            acc3[m, :, :, halves[side]] = total
        four[m] = []
        for off in range(1, Z):
            there = lax.rem(z + off, Z)
            k = m * (Z - 1) + off - 1
            s4[k] = acc3[m, there].astype(BF16)
            four[m].append((k, go(s4.at[k], r4.at[k], sem4, k, (there, p.lon))))

    for copy in returns:
        copy.wait_recv()
    cot_sum = cot_sums[:nodes] + back[0].astype(F32) + back[1].astype(F32)
    d_high, d_low = split_float(cot_sum * silu_slope(pre))
    hop_core(4, mm_t(mesh_out, d_high) + mm_t(mesh_out, d_low))
    d_node = (mm_nt(d_high, wd_ref[...]) * silu_slope(npre)).astype(BF16)
    hop_core(2, mm_t(agg, d_node))
    hop_first(4)
    c_high, c_low = split_float(d_node.astype(F32) * silu_slope(cpre))
    hop_core(3, mm_t(coarse_in, c_high) + mm_t(coarse_in, c_low))
    hop_first(2)
    d_edges = (mm_nt(d_node, wn_ref[...])[None] * silu_slope(edges_pre)).astype(BF16)
    d_sum = jnp.sum(d_edges.astype(F32), 0).astype(BF16)
    hop_core(1, mm_t(latent, d_sum))
    hop_first(3)
    hop_core(0, mm_t(beside, d_edges.reshape(slots * nodes, width)))
    hop_first(1)
    hop_first(0)
    order = (4, 2, 3, 1, 0)
    hop_other(order[0])
    for copy in spoken:
        copy.wait_recv()
    grid_ref[...] = (mm(cnt_high[...], msgs[...]) + mm(cnt_low[...], msgs[...])).astype(BF16)
    for m in order[1:]:
        hop_other(m)
    for m in order:
        hop_line(m)
    square = jnp.zeros(share.shape[1:], F32)
    for m in order:
        total = acc3[m, z]
        for k, copy in four[m]:
            copy.wait_recv()
            total = total + r4[k].astype(F32)
        share[m] = total
        square = square + total * total
    sq[0] = jnp.broadcast_to(jnp.sum(square, keepdims=True), sq.shape[1:])
    mine = []
    for off in range(1, Z):
        mine.append(go(sq.at[0], zq.at[off - 1], zsem, off - 1, (lax.rem(z + off, Z), p.lon)))
    whole = sq[0]
    for off, copy in enumerate(mine):
        copy.wait_recv()
        whole = whole + zq[off]
    sq[1] = whole
    mine = []
    for off in range(1, p.L):
        mine.append(go(sq.at[1], lq.at[off - 1], lsem, off - 1, (p.lat, lax.rem(p.lon + off, p.L))))
    for off, copy in enumerate(mine):
        copy.wait_recv()
        whole = whole + lq[off]
    norm = jnp.sqrt(whole[0:1, 0:1]) + 1e-06
    for m in range(many):
        total = share[m] / norm
        for r in range(R):
            out_ref[m:m + 1, r * width:(r + 1) * width] = total[r:r + 1]
    for copy in copies:
        copy.wait_send()


def run_step(sizes, latent, cot, weights, codes, ids, source, target, owner):
    Z, Y, X, C = sizes
    L = Y * X * C
    many = len(weights)
    nodes, width = latent.shape
    grid_rows = cot.shape[0]
    blocks, block_len = source.shape
    lanes = -(-3 * nodes // 128) * 128
    R = width // (Z * L)
    w2 = width // 2
    vmem = pl.BlockSpec(memory_space=pltpu.VMEM)

    def buf(dtype, *dims):
        return pltpu.VMEM(dims, dtype)

    def sems(*counts):
        return [pltpu.SemaphoreType.DMA((2, n)) for n in counts]

    nx, ny, nz, nc = many * (X - 1), many * (Y - 1), many * (Z - 1), many * (C - 1)
    second = [buf(BF16, nx, Z, Y, R, w2), buf(BF16, ny, Z, X, R, w2)]
    third = [buf(BF16, ny, Z, R, w2), buf(BF16, nx, Z, R, w2)]
    gathers = (Z - 1) * 2 + Z * (3 * (X - 1) + 3 * (Y - 1) + 2 * (C - 1))
    return pl.pallas_call(
        functools.partial(step_kernel, sizes),
        out_shape=(
            jax.ShapeDtypeStruct((nodes, width), BF16),
            jax.ShapeDtypeStruct((grid_rows, width), BF16),
            jax.ShapeDtypeStruct((many, R * width), F32),
        ),
        in_specs=[vmem] * (7 + many),
        out_specs=(vmem,) * 3,
        scratch_shapes=[
            buf(BF16, Z, Y, X, C, nodes, width), buf(jnp.int32, Z, Y, X, C, 1, C * nodes),
            buf(BF16, 9 * nodes, width), buf(jnp.int32, 4, 2, CAP, block_len),
            buf(jnp.int32, 2, blocks + 2 * CAP, block_len),
            buf(F32, grid_rows, lanes), buf(BF16, grid_rows, lanes), buf(BF16, grid_rows, lanes),
            buf(BF16, 2, nodes, width), buf(BF16, 2, nodes, width), buf(BF16, lanes, width),
            buf(F32, many, Z, Y, X, C, R, width),
            buf(BF16, nc, Z, Y, X, R, width), buf(BF16, nc, Z, Y, X, R, width),
            buf(F32, many, Z, Y, X, R, width),
            second, second, [buf(F32, many, Z, Y, R, w2), buf(F32, many, Z, X, R, w2)],
            third, third, buf(F32, many, Z, R, width),
            buf(BF16, nz, R, width), buf(BF16, nz, R, width),
            buf(F32, 2, 8, 128), buf(F32, Z - 1, 8, 128), buf(F32, L - 1, 8, 128),
            buf(jnp.int32, 1, C * nodes), buf(F32, many, R, width),
            *sems(gathers, 6, nc), sems(nx, ny), sems(ny, nx), *sems(nz, Z - 1, L - 1),
        ],
        compiler_params=pltpu.CompilerParams(
            collective_id=0, has_side_effects=True, vmem_limit_bytes=48 * 1024 * 1024
        ),
        name="whole_step",
    )(latent, cot, *weights, codes, ids, source, target, owner)


def write_kernel(*refs):
    count = len(refs) // 2
    sems = refs[-1]
    moves = [pltpu.make_async_copy(refs[i], refs[count + i], sems.at[i]) for i in range(count)]
    for move in moves:
        move.start()
    for move in moves:
        move.wait()


def write_results(*results):
    return pl.pallas_call(
        write_kernel,
        out_shape=tuple(jax.ShapeDtypeStruct(r.shape, r.dtype) for r in results),
        in_specs=[pl.BlockSpec(memory_space=pltpu.VMEM)] * len(results),
        out_specs=(pl.BlockSpec(memory_space=pl.ANY),) * len(results),
        scratch_shapes=[pltpu.SemaphoreType.DMA((len(results),))],
        compiler_params=pltpu.CompilerParams(vmem_limit_bytes=8 * 1024 * 1024),
        name="write_results",
    )(*results)


def lon_parts(lat_count, lon_count):
    chips = lon_count // 2
    x = next(d for d in range(math.isqrt(chips), 0, -1) if chips % d == 0)
    return lat_count, chips // x, x, 2


def local(
    mesh_latent,
    grid_cotangent,
    w_source,
    w_target,
    w_node,
    w_coarse,
    w_decode,
    neighbour_codes,
    coarse_ids,
    edge_source,
    edge_target,
    edge_owner,
):
    height, breadth, width = mesh_latent.shape
    nodes = height * breadth
    sizes = lon_parts(lax.axis_size("lat"), lax.axis_size("lon"))
    blocks = edge_owner.shape[0]
    mesh_out, grid_out, clipped = run_step(
        sizes,
        mesh_latent.reshape(nodes, width),
        grid_cotangent,
        (w_source, w_target, w_node, w_coarse, w_decode),
        neighbour_codes,
        coarse_ids.reshape(height, breadth),
        edge_source.reshape(blocks, -1),
        edge_target.reshape(blocks, -1),
        edge_owner.reshape(1, blocks),
    )
    mesh_out, grid_out, clipped = write_results(mesh_out, grid_out, clipped)
    return (mesh_out.reshape(height, breadth, width), grid_out, clipped)


def solution(mesh):
    in_specs = (
        P("lat", "lon", None),
        P(("lat", "lon"), None),
        P(),
        P(),
        P(),
        P(),
        P(),
        P(None, "lat", "lon"),
        P("lat", "lon", None),
        P(("lat", "lon")),
        P(("lat", "lon")),
        P(("lat", "lon"), None),
    )
    out_specs = (P("lat", "lon", None), P(("lat", "lon"), None), P(None, ("lat", "lon")))
    return jax.shard_map(local, mesh=mesh, in_specs=in_specs, out_specs=out_specs, check_vma=False)
```
